32 devices in a mesh: ctx: 4 (over z), head: 8 (over y, x, core).
Axes of the slice: x: 2, y: 2, z: 4, core: 2. Of those that a mesh axis runs over, the one named last changes fastest.
Arguments:
- query_rows: bfloat16 [8192, 4096], P('ctx', 'head'), may hold values from -6 to 6
- key_rows: bfloat16 [8192, 4096], P('ctx', 'head'), may hold values from -6 to 6
- value_rows: bfloat16 [8192, 4096], P('ctx', 'head'), may hold values from -6 to 6
- out_grad: bfloat16 [8192, 4096], P('ctx', 'head'), may hold values from -6 to 6
- hub_blocks: int32 [2], replicated, may hold values from 0 to 63, as said below
- local_lists: int32 [64, 6], replicated, may hold values from -3 to 3
Outputs:
- attended: bfloat16 [8192, 4096], P('ctx', 'head')
- query_gradient: bfloat16 [8192, 4096], P('ctx', 'head')
- key_grad: bfloat16 [8192, 4096], P('ctx', 'head')
- value_grad: bfloat16 [8192, 4096], P('ctx', 'head')
The draws below stay inside these ranges and needn't reach their ends.
Inputs may be any that keep to these rules, and one draw needn't show every extreme that they name: `hub_blocks`: 2 distinct block numbers.
All inputs are finite; a program needn't handle non-finite values.
Results may differ from the reference program's by a relative error of at most 0.012.
The reference program's roundings to bfloat16 on the way count: a program that leaves them out, or rounds other values in their place, can miss the bound.
Values may be sent and summed in bfloat16 or wider, within the bound.
A program may use at most 192 MiB of HBM per device.

```python
import math
import jax
import jax.numpy as jnp
from jax import lax

HEADS = 32
DH = 128
BLK = 128
HB = 3
LIST = 6
NBLK = 64
SEQ = 8192


def hub_pick(key):
    other_block = jax.random.randint(jax.random.fold_in(key, 11), (), 0, NBLK - 1).astype(jnp.int32)
    last_block = jnp.full((), NBLK - 1, dtype=jnp.int32)
    swapped = jax.random.randint(jax.random.fold_in(key, 12), (), 0, 2).astype(jnp.int32)
    first_hub = jnp.where(swapped == 1, other_block, last_block)
    second_hub = jnp.where(swapped == 1, last_block, other_block)
    return jnp.stack([first_hub, second_hub]).astype(jnp.int32)


def draw_hub_blocks(key, part):
    return hub_pick(key)


def draw_query_rows(key, part):
    background = jax.random.normal(jax.random.fold_in(key, 21), (SEQ, HEADS * DH), jnp.float32)
    return jnp.clip(background, -6.0, 6.0).astype(jnp.bfloat16)


def draw_key_rows(key, part):
    background = jax.random.normal(jax.random.fold_in(key, 22), (SEQ, HEADS * DH), jnp.float32)
    return jnp.clip(background, -6.0, 6.0).astype(jnp.bfloat16)


def place_ends(entries, rng, low, top_value):
    longest = entries.shape.index(max(entries.shape))
    spots = []
    for shift in (0, 1):
        where = [jax.random.randint(jax.random.fold_in(rng, axis), (), 0, length) for axis, length in enumerate(entries.shape)]
        where[longest] = (where[longest] + shift) % entries.shape[longest]
        spots.append(tuple(where))
    return entries.at[spots[0]].set(low).at[spots[1]].set(top_value)


def levels(key, dims, split, low, largest):
    def one(dim, parts):
        heights = jax.random.uniform(jax.random.fold_in(jax.random.fold_in(key, 6), dim), (parts,), jnp.float32, low / len(split), largest / len(split))
        return jnp.repeat(jnp.exp(heights), dims[dim] // parts).reshape((-1,) + (1,) * (len(dims) - dim - 1))

    loudness = one(*split[0])
    for cut in split[1:]:
        loudness = loudness * one(*cut)
    return loudness


def gaussian(rng, dims, scale, bound, cuts=(), kind=jnp.bfloat16):
    entries = scale * jax.random.normal(rng, dims, jnp.float32)
    if cuts:
        entries = entries * levels(rng, dims, cuts, -0.22, 0.18)
    return jnp.clip(entries, -bound, bound).astype(kind)


def setup_inputs(seed: int = 0) -> dict:
    keys = jax.random.split(jax.random.key(seed), 7)
    query_rows = draw_query_rows(jax.random.fold_in(keys[6], 71), 0)
    key_rows = draw_key_rows(jax.random.fold_in(keys[6], 71), 0)
    value_rows = gaussian(keys[2], (SEQ, HEADS * DH), 1.0, 6.0, ((0, 4), (1, 8)))
    out_grad = gaussian(keys[3], (SEQ, HEADS * DH), 1.0, 6.0, ((0, 4), (1, 8)))
    hub_blocks = draw_hub_blocks(jax.random.fold_in(keys[6], 71), 0)
    local_lists = place_ends(jax.random.randint(keys[5], (NBLK, LIST), 0 - HB, HB + 1), jax.random.fold_in(keys[5], 1), 0 - HB, HB).astype(jnp.int32)
    return dict(query_rows=query_rows, key_rows=key_rows, value_rows=value_rows, out_grad=out_grad, hub_blocks=hub_blocks, local_lists=local_lists)


def key_table(local_lists, hub_blocks):
    block_count = local_lists.shape[0]
    listed = jnp.arange(block_count, dtype=jnp.int32)[:, None] + local_lists.astype(jnp.int32)
    inside = (listed >= 0) & (listed < block_count)
    hub_cols = jnp.broadcast_to(hub_blocks.astype(jnp.int32)[None, :], (block_count, hub_blocks.shape[0]))
    table = jnp.concatenate([jnp.clip(listed, 0, block_count - 1), hub_cols], axis=1).astype(jnp.int32)
    living = jnp.concatenate([inside, jnp.ones(hub_cols.shape, dtype=bool)], axis=1)
    return (table, living)

def reference(query_rows, key_rows, value_rows, out_grad, hub_blocks, local_lists):
    score_scale = 1.0 / math.sqrt(DH)
    table, living = key_table(local_lists, hub_blocks)
    flat_table = table.reshape(-1)
    weight_keep_mask = living.astype(jnp.float32)[:, :, None, None]

    def split_heads(source):
        return jnp.transpose(source.reshape(NBLK, BLK, HEADS, DH), (2, 0, 1, 3))

    def join_heads(source):
        return jnp.transpose(source, (1, 2, 0, 3)).reshape(SEQ, HEADS * DH)

    def one_head(members):
        query_head, key_head, value_head, grad_head = members
        query_wide = query_head.astype(jnp.float32)
        gradient_wide = grad_head.astype(jnp.float32)
        key_block_set = key_head[table].astype(jnp.float32)
        value_block_set = value_head[table].astype(jnp.float32)
        logit_scores = jnp.einsum('ahw,amtw->ahmt', query_wide, key_block_set) * score_scale
        logit_scores = jnp.where(living[:, None, :, None], logit_scores, -1e+30)
        highest = lax.optimization_barrier(jnp.max(logit_scores, axis=(2, 3), keepdims=True))
        log_norm = highest + jnp.log(lax.optimization_barrier(jnp.sum(jnp.exp(logit_scores - highest), axis=(2, 3), keepdims=True)))
        chances = jnp.exp(logit_scores - log_norm)
        rounded_values = lax.optimization_barrier(chances.astype(jnp.bfloat16)).astype(jnp.float32)
        attended = jnp.einsum('nytu,ntua->nya', rounded_values, value_block_set).astype(jnp.bfloat16)
        offsets = lax.optimization_barrier(jnp.sum(gradient_wide * attended.astype(jnp.float32), axis=2))
        shifted_entries = jnp.einsum('ahw,amtw->ahmt', gradient_wide, value_block_set)
        decay_slopes = chances * (shifted_entries - offsets[:, :, None, None]) * score_scale
        decay_slopes = lax.optimization_barrier(decay_slopes.astype(jnp.bfloat16)).astype(jnp.float32)
        query_gradient = jnp.einsum('nytu,ntua->nya', decay_slopes, key_block_set).astype(jnp.bfloat16)
        key_pieces = jnp.einsum('fvil,fvw->filw', decay_slopes, query_wide) * weight_keep_mask
        value_pieces = jnp.einsum('fvil,fvw->filw', rounded_values, gradient_wide) * weight_keep_mask
        key_grad = jax.ops.segment_sum(key_pieces.reshape(-1, BLK, DH), flat_table, num_segments=NBLK)
        value_grad = jax.ops.segment_sum(value_pieces.reshape(-1, BLK, DH), flat_table, num_segments=NBLK)
        return (attended, query_gradient, key_grad.astype(jnp.bfloat16), value_grad.astype(jnp.bfloat16))
    attended, query_gradient, key_grad, value_grad = lax.map(one_head, (split_heads(query_rows), split_heads(key_rows), split_heads(value_rows), split_heads(out_grad)))
    return (join_heads(attended), join_heads(query_gradient), join_heads(key_grad), join_heads(value_grad))
```

```python
import functools
import math

import jax
import jax.numpy as jnp
from jax import lax
from jax.experimental import pallas as pl
from jax.experimental.pallas import tpu as pltpu
from jax.sharding import PartitionSpec as P

DH = 128
BLK = 128
HB = 3
G = 2
WIN = 2 * HB + 1
NE = WIN + G
RIM = HB * BLK
DEAD = -1e30
SCALE = 1.0 / math.sqrt(DH)
C = SCALE * math.log2(math.e)
F32 = jnp.float32
BF = jnp.bfloat16
MESH = pl.DeviceIdType.MESH
ENTRY = [slice(e * BLK, (e + 1) * BLK) for e in range(NE)]


def dot(a, b):
    return jnp.dot(a, b, preferred_element_type=F32)


def fold(x, op):
    return op(x.reshape(x.shape[0] // 8, 8, x.shape[1]), axis=0)


def rows_of(b, n=1):
    return pl.ds(pl.multiple_of(b * BLK, BLK), n * BLK)


def cols_of(h):
    return pl.ds(pl.multiple_of(h * DH, DH), DH)


def layer_kernel(
    hub_ref, lists_ref, q_ref, k_ref, v_ref, g_ref, att_out, dq_out, dk_out, dv_out,
    kx, vx, qx, gx, kt, vt, qt, gt, dka, dva, bias, att, dq, dk, dv,
    hub_own, hub_fl, hub_fr, hub_tr, hub_tl,
    hg_own, hg_fl, hg_fr, hg_tr, hg_tl, hub_sum,
    rim_tl, rim_tr, rim_fl, rim_fr,
    s0, s1, p0, p1, m0, m1, w0, w1, l0, l1,
    load_sem, store_sem, rim_send, rim_recv, hub_send, hub_recv,
    back_send, back_recv, hg_send, hg_recv,
):
    heads, tokens, _ = qx.shape
    blocks = tokens // BLK
    extended = blocks + 2 * HB
    half = blocks // 2
    me = lax.axis_index("ctx")
    last = lax.axis_size("ctx") - 1
    own = pl.ds(RIM, tokens)
    hubs = slice(extended * BLK, (extended + G) * BLK)
    right_rim = slice((HB + blocks) * BLK, extended * BLK)
    S, PU, M, W, L = (s0, s1), (p0, p1), (m0, m1), (w0, w1), (l0, l1)

    def loads(h):
        pairs = ((k_ref, kx.at[h, own]), (v_ref, vx.at[h, own]), (q_ref, qx.at[h]), (g_ref, gx.at[h]))
        return [
            pltpu.make_async_copy(src.at[:, cols_of(h)], dst, load_sem.at[i, h])
            for i, (src, dst) in enumerate(pairs)
        ]

    def stores(h):
        pairs = ((att, att_out), (dq, dq_out), (dk, dk_out), (dv, dv_out))
        return [
            pltpu.make_async_copy(src.at[h], dst.at[:, cols_of(h)], store_sem.at[i, h])
            for i, (src, dst) in enumerate(pairs)
        ]

    def remote(src, dst, send, recv, to):
        return pltpu.make_async_remote_copy(
            src_ref=src, dst_ref=dst, send_sem=send, recv_sem=recv,
            device_id={"ctx": to}, device_id_type=MESH,
        )

    def rims(h, right):
        source = pl.ds(tokens - RIM, RIM) if right else pl.ds(0, RIM)
        target = pl.ds(0, RIM) if right else right_rim
        d = 0 if right else 1
        to = me + 1 if right else me - 1
        return [
            remote(a.at[source, cols_of(h)], x.at[h, target], rim_send.at[d, i, h], rim_recv.at[d, i, h], to)
            for i, (a, x) in enumerate(((k_ref, kx), (v_ref, vx)))
        ]

    def backs(h, right):
        if right:
            return remote(rim_tr.at[h], rim_fl.at[h], back_send.at[0, h], back_recv.at[0, h], me + 1)
        return remote(rim_tl.at[h], rim_fr.at[h], back_send.at[1, h], back_recv.at[1, h], me - 1)

    hub_in = (hub_own, hub_fl, hub_fr, hub_tr, hub_tl, hub_send, hub_recv)
    hub_back = (hg_own, hg_fl, hg_fr, hg_tr, hg_tl, hg_send, hg_recv)

    def hop(chain, h, right, source=None):
        mine, fl, fr, tr, tl, send, recv = chain
        if right:
            return remote((tr if source is None else source).at[h], fl.at[h], send.at[0, h], recv.at[0, h], me + 1)
        return remote((tl if source is None else source).at[h], fr.at[h], send.at[1, h], recv.at[1, h], me - 1)

    def step(chain, h, right):
        mine, fl, fr, tr, tl = chain[:5]
        first, final = (0, last) if right else (last, 0)

        @pl.when(me == first)
        def _():
            hop(chain, h, right, mine).start()

        @pl.when(me != first)
        def _():
            hop(chain, h, right).wait_recv()

        @pl.when((me != first) & (me != final))
        def _():
            if right:
                tr[h] = mine[h] + fl[h]
            else:
                tl[h] = mine[h] + fr[h]
            hop(chain, h, right).start()

    def near(chain, h):
        @pl.when(me <= last - me)
        def _():
            step(chain, h, True)

        @pl.when(me > last - me)
        def _():
            step(chain, h, False)

    def far(chain, h):
        @pl.when(me <= last - me)
        def _():
            step(chain, h, False)

        @pl.when(me > last - me)
        def _():
            step(chain, h, True)

    def chain_total(chain, h):
        mine, fl, fr = chain[:3]
        total = mine[h].astype(F32)
        total = total + jnp.where(me > 0, fl[h].astype(F32), 0.0)
        return total + jnp.where(me < last, fr[h].astype(F32), 0.0)

    def on_block(b):
        return [jnp.where(hub_ref[j] - me * blocks == b, 1.0, 0.0).astype(F32) for j in range(G)]

    def send_rims(h):
        @pl.when(me < last)
        def _():
            for copy in rims(h, True):
                copy.start()

        @pl.when(me > 0)
        def _():
            for copy in rims(h, False):
                copy.start()

    def pick(h):
        def add(b, sums):
            ons = on_block(b)
            out = []
            for i, x in enumerate((kx, vx)):
                rows = x[h, rows_of(HB + b), :].astype(F32)
                out += [sums[G * i + j] + ons[j] * rows for j in range(G)]
            return tuple(out)

        zero = jnp.zeros((BLK, DH), F32)
        sums = lax.fori_loop(0, blocks, add, (zero,) * (2 * G))
        for i in range(2):
            for j in range(G):
                hub_own[h, i, ENTRY[j], :] = sums[G * i + j].astype(BF)

    def turn(h, slot, b):
        r = rows_of(b)
        e = rows_of(HB + b)
        qt[slot, b] = qx[h, r, :].T
        gt[slot, b] = gx[h, r, :].T
        kt[slot, :, e] = kx[h, e, :].T
        vt[slot, :, e] = vx[h, e, :].T

    def assemble(h):
        @pl.when(me > 0)
        def _():
            for copy in rims(h, True):
                copy.wait_recv()

        @pl.when(me == 0)
        def _():
            kx[h, 0:RIM, :] = jnp.zeros((RIM, DH), BF)
            vx[h, 0:RIM, :] = jnp.zeros((RIM, DH), BF)

        @pl.when(me < last)
        def _():
            for copy in rims(h, False):
                copy.wait_recv()

        @pl.when(me == last)
        def _():
            kx[h, right_rim, :] = jnp.zeros((RIM, DH), BF)
            vx[h, right_rim, :] = jnp.zeros((RIM, DH), BF)

        mine, fl, fr = hub_in[:3]
        for i, x in enumerate((kx, vx)):
            total = mine[h, i]
            total = total + jnp.where(me > 0, fl[h, i], jnp.zeros_like(total))
            total = total + jnp.where(me < last, fr[h, i], jnp.zeros_like(total))
            x[h, hubs, :] = total
        slot = h % 2
        for x, t in ((kx, kt), (vx, vt)):
            for e in list(range(HB)) + list(range(HB + blocks, extended + G)):
                es = slice(e * BLK, (e + 1) * BLK)
                t[slot, :, es] = x[h, es, :].T

    def scores(h, b, n):
        slot = h % 2
        qt_b, gt_b = qt[slot, b], gt[slot, b]
        window = rows_of(b, WIN)
        s_local = dot(kx[h, window, :], qt_b)
        s_hub = dot(kx[h, hubs, :], qt_b)
        S[n][: WIN * BLK, :] = s_local
        S[n][WIN * BLK :, :] = s_hub
        PU[n][: WIN * BLK, :] = dot(vx[h, window, :], gt_b)
        PU[n][WIN * BLK :, :] = dot(vx[h, hubs, :], gt_b)
        tops = [fold(s_local[ENTRY[e]], jnp.max) * C + bias[b, e] for e in range(WIN)]
        tops += [fold(s_hub[ENTRY[e]], jnp.max) * C for e in range(G)]
        M[n][...] = functools.reduce(jnp.maximum, tops)

    def softmax(b, n):
        shift = [bias[b, e] for e in range(WIN)] + [0.0] * G
        top = jnp.max(M[n][...], axis=0, keepdims=True)
        ps = [jnp.exp2(S[n][ENTRY[e], :] * C + (shift[e] - top)) for e in range(NE)]
        total = functools.reduce(jnp.add, [fold(p, jnp.sum) for p in ps])
        moved = functools.reduce(
            jnp.add, [fold(ps[e] * PU[n][ENTRY[e], :], jnp.sum) for e in range(NE)]
        )
        inverse = 1.0 / jnp.sum(total, axis=0, keepdims=True)
        offset = jnp.sum(moved, axis=0, keepdims=True) * inverse
        for e in range(NE):
            chances = ps[e] * inverse
            W[n][ENTRY[e], :] = chances.astype(BF)
            L[n][ENTRY[e], :] = (chances * (PU[n][ENTRY[e], :] - offset)).astype(BF)

    def products(h, b, n):
        slot = h % 2
        r = rows_of(b)
        window = rows_of(b, WIN)
        local = slice(0, WIN * BLK)
        hub = slice(WIN * BLK, NE * BLK)
        mixed = dot(vt[slot, :, window], W[n][local, :]) + dot(vt[slot, :, hubs], W[n][hub, :])
        att[h, r, :] = mixed.T.astype(BF)
        grad = dot(kt[slot, :, window], L[n][local, :]) + dot(kt[slot, :, hubs], L[n][hub, :])
        dq[h, r, :] = (grad * SCALE).T.astype(BF)
        a = dot(L[n][...], qx[h, r, :])
        d = dot(W[n][...], gx[h, r, :])
        dka[window, :] += a[local]
        dka[hubs, :] += a[hub]
        dva[window, :] += d[local]
        dva[hubs, :] += d[hub]

    def clear():
        dka[...] = jnp.zeros(dka.shape, F32)
        dva[...] = jnp.zeros(dva.shape, F32)

    def deliver(h):
        for i, (acc, scale) in enumerate(((dka, SCALE), (dva, 1.0))):
            rim_tl[h, i] = (acc[0:RIM, :] * scale).astype(BF)
            rim_tr[h, i] = (acc[right_rim, :] * scale).astype(BF)
            hg_own[h, i] = (acc[hubs, :] * scale).astype(BF)

        @pl.when(me < last)
        def _():
            backs(h, True).start()

        @pl.when(me > 0)
        def _():
            backs(h, False).start()

        def keep(b, carry):
            dk[h, rows_of(b), :] = (dka[rows_of(HB + b), :] * SCALE).astype(BF)
            dv[h, rows_of(b), :] = dva[rows_of(HB + b), :].astype(BF)
            return carry

        lax.fori_loop(0, blocks, keep, 0)
        clear()
        for copy in stores(h)[:2]:
            copy.start()

    def finish(h):
        @pl.when(me > 0)
        def _():
            backs(h, True).wait_recv()
            for i, x in enumerate((dk, dv)):
                x[h, 0:RIM, :] = (x[h, 0:RIM, :].astype(F32) + rim_fl[h, i].astype(F32)).astype(BF)

        @pl.when(me < last)
        def _():
            backs(h, False).wait_recv()
            end = slice(tokens - RIM, tokens)
            for i, x in enumerate((dk, dv)):
                x[h, end, :] = (x[h, end, :].astype(F32) + rim_fr[h, i].astype(F32)).astype(BF)

        hub_sum[...] = chain_total(hub_back, h)

        def add(b, carry):
            ons = on_block(b)
            for i, x in enumerate((dk, dv)):
                out = x[h, rows_of(b), :].astype(F32)
                for j in range(G):
                    out = out + ons[j] * hub_sum[i, ENTRY[j], :]
                x[h, rows_of(b), :] = out.astype(BF)
            return carry

        lax.fori_loop(0, blocks, add, 0)
        for copy in stores(h)[2:]:
            copy.start()

    def table(b, carry):
        listed = lists_ref.shape[1]
        at = me * blocks + b
        for e in range(WIN):
            r = e - HB
            count = jnp.int32(0)
            for j in range(listed):
                count = count + jnp.where(lists_ref[at, j] == r, 1, 0)
            alive = (at + r >= 0) & (at + r < blocks * (last + 1))
            value = jnp.float32(DEAD)
            for n in range(1, listed + 1):
                value = jnp.where(alive & (count == n), jnp.float32(math.log2(n)), value)
            bias[b, e] = value
        return carry

    barrier = pltpu.get_barrier_semaphore()

    @pl.when(me > 0)
    def _():
        pl.semaphore_signal(barrier, inc=1, device_id={"ctx": me - 1}, device_id_type=MESH)

    @pl.when(me < last)
    def _():
        pl.semaphore_signal(barrier, inc=1, device_id={"ctx": me + 1}, device_id_type=MESH)

    def load_all(h, carry):
        for copy in loads(h):
            copy.start()
        return carry

    lax.fori_loop(0, heads, load_all, 0)

    @pl.when((me > 0) & (me < last))
    def _():
        pl.semaphore_wait(barrier, 2)

    @pl.when((me == 0) | (me == last))
    def _():
        pl.semaphore_wait(barrier, 1)

    def start_head(h):
        for copy in loads(h):
            copy.wait()
        pick(h)
        send_rims(h)

    start_head(0)
    near(hub_in, 0)
    lax.fori_loop(0, blocks, table, 0)

    def turn_first(b, carry):
        turn(0, 0, b)
        return carry

    lax.fori_loop(0, blocks, turn_first, 0)
    far(hub_in, 0)
    clear()
    assemble(0)
    scores(0, 0, 0)
    softmax(0, 0)
    scores(0, 1, 1)

    right_at = jnp.minimum(me, half - 2)
    left_at = jnp.minimum(last - me, half - 2)

    def head(h, carry):
        more = h + 1 < heads
        ahead = jnp.minimum(h + 1, heads - 1)

        @pl.when(more)
        def _():
            start_head(h + 1)

        def pair(i, carry):
            @pl.when(more & (i == right_at))
            def _():
                step(hub_in, h + 1, True)

            @pl.when(more & (i == left_at))
            def _():
                step(hub_in, h + 1, False)

            @pl.when((h > 0) & (i == right_at))
            def _():
                step(hub_back, h - 1, True)

            @pl.when((h > 0) & (i == left_at))
            def _():
                step(hub_back, h - 1, False)

            @pl.when((h > 0) & (i == half - 1))
            def _():
                finish(h - 1)

            @pl.when(more)
            def _():
                turn(h + 1, (h + 1) % 2, 2 * i)
                turn(h + 1, (h + 1) % 2, 2 * i + 1)

            @pl.when(more & (i == half - 1))
            def _():
                assemble(h + 1)

            b = 2 * i
            ends = i == half - 1
            h_next = jnp.where(ends, ahead, h)
            b_next = jnp.where(ends, 0, b + 2)
            scores(h_next, b_next, 0)
            softmax(b + 1, 1)
            products(h, b, 0)
            scores(h_next, b_next + 1, 1)
            softmax(b_next, 0)
            products(h, b + 1, 1)
            return carry

        lax.fori_loop(0, half, pair, 0)
        deliver(h)
        return carry

    lax.fori_loop(0, heads, head, 0)
    near(hub_back, heads - 1)
    far(hub_back, heads - 1)
    finish(heads - 1)

    def close(h, carry):
        for copy in stores(h):
            copy.wait()

        @pl.when(me < last)
        def _():
            for copy in rims(h, True):
                copy.wait_send()
            backs(h, True).wait_send()
            hop(hub_in, h, True).wait_send()
            hop(hub_back, h, True).wait_send()

        @pl.when(me > 0)
        def _():
            for copy in rims(h, False):
                copy.wait_send()
            backs(h, False).wait_send()
            hop(hub_in, h, False).wait_send()
            hop(hub_back, h, False).wait_send()

        return carry

    lax.fori_loop(0, heads, close, 0)


def local(query_rows, key_rows, value_rows, out_grad, hub_blocks, local_lists):
    tokens, columns = query_rows.shape
    heads = columns // DH
    store = tokens + 2 * RIM + G * BLK
    blocks = tokens // BLK
    big = jax.ShapeDtypeStruct(query_rows.shape, BF)
    anywhere = pl.BlockSpec(memory_space=pl.ANY)
    smem = pl.BlockSpec(memory_space=pltpu.SMEM)
    vmem = pltpu.VMEM
    hub_shape = vmem((heads, 2, G * BLK, DH), BF)
    rim_shape = vmem((heads, 2, RIM, DH), BF)
    dma = pltpu.SemaphoreType.DMA
    units = 6 * heads * blocks * NE
    return pl.pallas_call(
        layer_kernel,
        out_shape=[big] * 4,
        in_specs=[smem] * 2 + [anywhere] * 4,
        out_specs=[anywhere] * 4,
        scratch_shapes=[vmem((heads, store, DH), BF)] * 2
        + [vmem((heads, tokens, DH), BF)] * 2
        + [vmem((2, DH, store), BF)] * 2
        + [vmem((2, blocks, DH, BLK), BF)] * 2
        + [vmem((store, DH), F32)] * 2
        + [pltpu.SMEM((blocks, 8), F32)]
        + [vmem((heads, tokens, DH), BF)] * 4
        + [hub_shape] * 10
        + [vmem((2, G * BLK, DH), F32)]
        + [rim_shape] * 4
        + [vmem((NE * BLK, BLK), F32)] * 4
        + [vmem((8, BLK), F32)] * 2
        + [vmem((NE * BLK, BLK), BF)] * 4
        + [dma((4, heads))] * 2
        + [dma((2, 2, heads))] * 2
        + [dma((2, heads))] * 6,
        compiler_params=pltpu.CompilerParams(
            collective_id=0, has_side_effects=True, vmem_limit_bytes=56 << 20
        ),
        cost_estimate=pl.CostEstimate(
            flops=units * 2 * BLK * BLK * DH,
            bytes_accessed=16 * tokens * columns,
            transcendentals=heads * blocks * NE * BLK * BLK,
        ),
        name="layer",
    )(hub_blocks, local_lists, query_rows, key_rows, value_rows, out_grad)


def solution(mesh):
    spec = P("ctx", "head")
    return jax.shard_map(
        local,
        mesh=mesh,
        in_specs=(spec, spec, spec, spec, P(), P()),
        out_specs=(spec, spec, spec, spec),
        check_vma=False,
    )
```

```python
import functools
import math

import jax
import jax.numpy as jnp
from jax import lax
from jax.experimental import pallas as pl
from jax.experimental.pallas import tpu as pltpu
from jax.sharding import PartitionSpec as P

DH = 128
BLK = 128
HB = 3
G = 2
WIN = 2 * HB + 1
NE = WIN + G
RIM = HB * BLK
DEAD = -1e30
PARTS = 1
IN_AT, IN_GAP = 1, 2
BACK_AT, BACK_GAP = 3, 2
SCALE = 1.0 / math.sqrt(DH)
C = SCALE * math.log2(math.e)
F32 = jnp.float32
BF = jnp.bfloat16
MESH = pl.DeviceIdType.MESH
ENTRY = [slice(e * BLK, (e + 1) * BLK) for e in range(NE)]


def dot(a, b):
    return jnp.dot(a, b, preferred_element_type=F32)


def fold(x, op):
    return op(x.reshape(x.shape[0] // 8, 8, x.shape[1]), axis=0)


def rows_of(b, n=1):
    return pl.ds(pl.multiple_of(b * BLK, BLK), n * BLK)


def cols_of(h):
    return pl.ds(pl.multiple_of(h * DH, DH), DH)


def layer_kernel(
    hub_ref, lists_ref, q_ref, k_ref, v_ref, g_ref, k3_ref, v3_ref, att_out, dq_out, dk_out, dv_out,
    kx, vx, qx, gx, ko, vo, kt, vt, qt, gt, dka, dva, bias, att, dq, dk, dv,
    hub_own, hub_fl, hub_fr, hub_tr, hub_tl,
    hg_own, hg_fl, hg_fr, hg_tr, hg_tl, hub_sum,
    rim_tl, rim_tr, rim_fl, rim_fr,
    s0, s1, p0, p1, m0, m1, w0, w1, l0, l1,
    whole_sem, load_sem, store_sem, rim_send, rim_recv, hub_send, hub_recv,
    back_send, back_recv, hg_send, hg_recv,
):
    heads, tokens, _ = qx.shape
    blocks = tokens // BLK
    extended = blocks + 2 * HB
    half = blocks // 2
    me = lax.axis_index("ctx")
    last = lax.axis_size("ctx") - 1
    own = pl.ds(RIM, tokens)
    hubs = slice(extended * BLK, (extended + G) * BLK)
    right_rim = slice((HB + blocks) * BLK, extended * BLK)
    S, PU, M, W, L = (s0, s1), (p0, p1), (m0, m1), (w0, w1), (l0, l1)

    def loads(h):
        pairs = (
            (k_ref, kx.at[h, own]), (v_ref, vx.at[h, own]),
            (q_ref, qx.at[h]), (g_ref, gx.at[h]),
        )
        return [
            pltpu.make_async_copy(src.at[:, cols_of(h)], dst, load_sem.at[i, h])
            for i, (src, dst) in enumerate(pairs)
        ]

    def wholes():
        return [
            pltpu.make_async_copy(src, dst, whole_sem.at[i])
            for i, (src, dst) in enumerate(((k3_ref, ko), (v3_ref, vo)))
        ]

    def stores(h, which=range(4)):
        pairs = ((att, att_out), (dq, dq_out), (dk, dk_out), (dv, dv_out))
        return [
            pltpu.make_async_copy(src.at[h], dst.at[:, cols_of(h)], store_sem.at[i, h])
            for i, (src, dst) in enumerate(pairs)
            if i in which
        ]

    def remote(src, dst, send, recv, to):
        return pltpu.make_async_remote_copy(
            src_ref=src, dst_ref=dst, send_sem=send, recv_sem=recv,
            device_id={"ctx": to}, device_id_type=MESH,
        )

    def rims(h, right):
        source = pl.ds(blocks * BLK, RIM) if right else pl.ds(RIM, RIM)
        target = pl.ds(0, RIM) if right else right_rim
        d = 0 if right else 1
        to = me + 1 if right else me - 1
        return [
            remote(x.at[h, source], x.at[h, target], rim_send.at[d, i, h], rim_recv.at[d, i, h], to)
            for i, x in enumerate((kx, vx))
        ]

    def backs(h, right):
        if right:
            return remote(rim_tr.at[h], rim_fl.at[h], back_send.at[0, h], back_recv.at[0, h], me + 1)
        return remote(rim_tl.at[h], rim_fr.at[h], back_send.at[1, h], back_recv.at[1, h], me - 1)

    hub_in = (hub_own, hub_fl, hub_fr, hub_tr, hub_tl, hub_send, hub_recv)
    hub_back = (hg_own, hg_fl, hg_fr, hg_tr, hg_tl, hg_send, hg_recv)

    def hop(chain, h, right, i, source=None):
        mine, fl, fr, tr, tl, send, recv = chain
        d = 0 if right else 1
        land, to = (fl, me + 1) if right else (fr, me - 1)
        if source is None:
            source = tr if right else tl
        return remote(source.at[h, i], land.at[h, i], send.at[d, i, h], recv.at[d, i, h], to)

    def step(chain, h, right):
        mine, fl, fr, tr, tl = chain[:5]
        first, final = (0, last) if right else (last, 0)
        got, sent = (fl, tr) if right else (fr, tl)
        for i in range(2):
            @pl.when(me == first)
            def _():
                hop(chain, h, right, i, mine).start()

            @pl.when(me != first)
            def _():
                hop(chain, h, right, i).wait_recv()

            @pl.when((me != first) & (me != final))
            def _():
                sent[h, i] = mine[h, i] + got[h, i]
                hop(chain, h, right, i).start()

    def near(chain, h):
        @pl.when(me <= last - me)
        def _():
            step(chain, h, True)

        @pl.when(me > last - me)
        def _():
            step(chain, h, False)

    def far(chain, h):
        @pl.when(me <= last - me)
        def _():
            step(chain, h, False)

        @pl.when(me > last - me)
        def _():
            step(chain, h, True)

    def chain_total(chain, h):
        mine, fl, fr = chain[:3]
        total = mine[h].astype(F32)
        total = total + jnp.where(me > 0, fl[h].astype(F32), 0.0)
        return total + jnp.where(me < last, fr[h].astype(F32), 0.0)

    def on_block(b):
        return [jnp.where(hub_ref[j] - me * blocks == b, 1.0, 0.0).astype(F32) for j in range(G)]

    def send_rims(h):
        @pl.when(me < last)
        def _():
            for copy in rims(h, True):
                copy.start()

        @pl.when(me > 0)
        def _():
            for copy in rims(h, False):
                copy.start()

    def pick():
        for j in range(G):
            spot = hub_ref[j] - me * blocks
            here = jnp.where((spot >= 0) & (spot < blocks), 1.0, 0.0).astype(F32)
            at = jnp.clip(spot, 0, blocks - 1)
            for i, x in enumerate((ko, vo)):
                block = (x[at].astype(F32) * here).astype(BF)
                for h in range(heads):
                    hub_own[h, i, ENTRY[j], :] = block[:, h * DH : (h + 1) * DH]

    def turn(h, slot, b):
        r = rows_of(b)
        e = rows_of(HB + b)
        qt[slot, b] = qx[h, r, :].T
        gt[slot, b] = gx[h, r, :].T
        kt[slot, :, e] = kx[h, e, :].T
        vt[slot, :, e] = vx[h, e, :].T

    def assemble(h):
        @pl.when(me > 0)
        def _():
            for copy in rims(h, True):
                copy.wait_recv()

        @pl.when(me == 0)
        def _():
            kx[h, 0:RIM, :] = jnp.zeros((RIM, DH), BF)
            vx[h, 0:RIM, :] = jnp.zeros((RIM, DH), BF)

        @pl.when(me < last)
        def _():
            for copy in rims(h, False):
                copy.wait_recv()

        @pl.when(me == last)
        def _():
            kx[h, right_rim, :] = jnp.zeros((RIM, DH), BF)
            vx[h, right_rim, :] = jnp.zeros((RIM, DH), BF)

        mine, fl, fr = hub_in[:3]
        for i, x in enumerate((kx, vx)):
            total = mine[h, i]
            total = total + jnp.where(me > 0, fl[h, i], jnp.zeros_like(total))
            total = total + jnp.where(me < last, fr[h, i], jnp.zeros_like(total))
            x[h, hubs, :] = total
        slot = h % 2
        for x, t in ((kx, kt), (vx, vt)):
            for e in list(range(HB)) + list(range(HB + blocks, extended + G)):
                es = slice(e * BLK, (e + 1) * BLK)
                t[slot, :, es] = x[h, es, :].T

    def scores(h, b, n):
        slot = h % 2
        qt_b, gt_b = qt[slot, b], gt[slot, b]
        window = rows_of(b, WIN)
        s_local = dot(kx[h, window, :], qt_b)
        s_hub = dot(kx[h, hubs, :], qt_b)
        S[n][: WIN * BLK, :] = s_local
        S[n][WIN * BLK :, :] = s_hub
        PU[n][: WIN * BLK, :] = dot(vx[h, window, :], gt_b)
        PU[n][WIN * BLK :, :] = dot(vx[h, hubs, :], gt_b)
        tops = [fold(s_local[ENTRY[e]], jnp.max) * C + bias[b, e] for e in range(WIN)]
        tops += [fold(s_hub[ENTRY[e]], jnp.max) * C for e in range(G)]
        M[n][...] = functools.reduce(jnp.maximum, tops)

    def softmax(b, n):
        shift = [bias[b, e] for e in range(WIN)] + [0.0] * G
        top = jnp.max(M[n][...], axis=0, keepdims=True)
        ps = [jnp.exp2(S[n][ENTRY[e], :] * C + (shift[e] - top)) for e in range(NE)]
        total = functools.reduce(jnp.add, [fold(p, jnp.sum) for p in ps])
        moved = functools.reduce(
            jnp.add, [fold(ps[e] * PU[n][ENTRY[e], :], jnp.sum) for e in range(NE)]
        )
        inverse = 1.0 / jnp.sum(total, axis=0, keepdims=True)
        offset = jnp.sum(moved, axis=0, keepdims=True) * inverse
        for e in range(NE):
            chances = ps[e] * inverse
            W[n][ENTRY[e], :] = chances.astype(BF)
            L[n][ENTRY[e], :] = (chances * (PU[n][ENTRY[e], :] - offset)).astype(BF)

    def products(h, b, n):
        slot = h % 2
        r = rows_of(b)
        window = rows_of(b, WIN)
        local = slice(0, WIN * BLK)
        hub = slice(WIN * BLK, NE * BLK)
        mixed = dot(vt[slot, :, window], W[n][local, :]) + dot(vt[slot, :, hubs], W[n][hub, :])
        att[h, r, :] = mixed.T.astype(BF)
        grad = dot(kt[slot, :, window], L[n][local, :]) + dot(kt[slot, :, hubs], L[n][hub, :])
        dq[h, r, :] = (grad * SCALE).T.astype(BF)
        a = dot(L[n][...], qx[h, r, :])
        d = dot(W[n][...], gx[h, r, :])
        dka[window, :] += a[local]
        dka[hubs, :] += a[hub]
        dva[window, :] += d[local]
        dva[hubs, :] += d[hub]

    def clear():
        dka[...] = jnp.zeros(dka.shape, F32)
        dva[...] = jnp.zeros(dva.shape, F32)

    def deliver(h):
        for i, (acc, scale) in enumerate(((dka, SCALE), (dva, 1.0))):
            rim_tl[h, i] = (acc[0:RIM, :] * scale).astype(BF)
            rim_tr[h, i] = (acc[right_rim, :] * scale).astype(BF)
            hg_own[h, i] = (acc[hubs, :] * scale).astype(BF)

        @pl.when(me < last)
        def _():
            backs(h, True).start()

        @pl.when(me > 0)
        def _():
            backs(h, False).start()

        def keep(b, carry):
            dk[h, rows_of(b), :] = (dka[rows_of(HB + b), :] * SCALE).astype(BF)
            dv[h, rows_of(b), :] = dva[rows_of(HB + b), :].astype(BF)
            return carry

        lax.fori_loop(0, blocks, keep, 0)
        clear()
        for copy in stores(h, (0, 1)):
            copy.start()

    def finish(h):
        @pl.when(me > 0)
        def _():
            backs(h, True).wait_recv()
            for i, x in enumerate((dk, dv)):
                x[h, 0:RIM, :] = (x[h, 0:RIM, :].astype(F32) + rim_fl[h, i].astype(F32)).astype(BF)

        @pl.when(me < last)
        def _():
            backs(h, False).wait_recv()
            end = slice(tokens - RIM, tokens)
            for i, x in enumerate((dk, dv)):
                x[h, end, :] = (x[h, end, :].astype(F32) + rim_fr[h, i].astype(F32)).astype(BF)

        hub_sum[...] = chain_total(hub_back, h)

        def add(b, carry):
            ons = on_block(b)
            for i, x in enumerate((dk, dv)):
                out = x[h, rows_of(b), :].astype(F32)
                for j in range(G):
                    out = out + ons[j] * hub_sum[i, ENTRY[j], :]
                x[h, rows_of(b), :] = out.astype(BF)
            return carry

        lax.fori_loop(0, blocks, add, 0)
        for copy in stores(h, (2, 3)):
            copy.start()

    def table(b, carry):
        listed = lists_ref.shape[0]
        at = me * blocks + b
        for e in range(WIN):
            r = e - HB
            count = jnp.int32(0)
            for j in range(listed):
                count = count + jnp.where(lists_ref[j, at] == r, 1, 0)
            alive = (at + r >= 0) & (at + r < blocks * (last + 1))
            value = jnp.float32(DEAD)
            for n in range(1, listed + 1):
                value = jnp.where(alive & (count == n), jnp.float32(math.log2(n)), value)
            bias[b, e] = value
        return carry

    barrier = pltpu.get_barrier_semaphore()

    @pl.when(me > 0)
    def _():
        pl.semaphore_signal(barrier, inc=1, device_id={"ctx": me - 1}, device_id_type=MESH)

    @pl.when(me < last)
    def _():
        pl.semaphore_signal(barrier, inc=1, device_id={"ctx": me + 1}, device_id_type=MESH)

    for copy in wholes():
        copy.start()

    def load_all(h, carry):
        for copy in loads(h):
            copy.start()
        return carry

    lax.fori_loop(0, heads, load_all, 0)

    @pl.when((me > 0) & (me < last))
    def _():
        pl.semaphore_wait(barrier, 2)

    @pl.when((me == 0) | (me == last))
    def _():
        pl.semaphore_wait(barrier, 1)

    def open_head(h):
        for copy in loads(h):
            copy.wait()

    def lead(h):
        @pl.when(me == 0)
        def _():
            step(hub_in, h, True)

        @pl.when(me == last)
        def _():
            step(hub_in, h, False)

    for copy in wholes():
        copy.wait()
    pick()
    near(hub_in, 0)
    open_head(0)
    send_rims(0)
    lax.fori_loop(0, blocks, table, 0)

    def turn_first(b, carry):
        turn(0, 0, b)
        return carry

    lax.fori_loop(0, blocks, turn_first, 0)
    far(hub_in, 0)
    if heads > 1:
        open_head(1)
        lead(1)
        send_rims(1)
    clear()
    assemble(0)
    scores(0, 0, 0)
    softmax(0, 0)
    scores(0, 1, 1)

    rank, knar = me, last - me
    in_right = jnp.where(rank > 0, jnp.minimum(IN_GAP * (rank - 1) + IN_AT, half - 2), -1)
    in_left = jnp.where(knar > 0, jnp.minimum(IN_GAP * (knar - 1) + IN_AT, half - 2), -1)
    back_right = jnp.where(rank > 0, jnp.minimum(BACK_GAP * (rank - 1) + BACK_AT, half - 1), 0)
    back_left = jnp.where(knar > 0, jnp.minimum(BACK_GAP * (knar - 1) + BACK_AT, half - 1), 0)

    def head(h, carry):
        more = h + 1 < heads
        ahead = jnp.minimum(h + 1, heads - 1)

        def pair(i, carry):
            @pl.when(more & (i == in_right))
            def _():
                step(hub_in, h + 1, True)

            @pl.when(more & (i == in_left))
            def _():
                step(hub_in, h + 1, False)

            @pl.when((h > 0) & (i == back_right))
            def _():
                step(hub_back, h - 1, True)

            @pl.when((h > 0) & (i == back_left))
            def _():
                step(hub_back, h - 1, False)

            @pl.when((h > 1) & (i == half // 2 - 1))
            def _():
                finish(h - 2)

            @pl.when((h + 2 < heads) & (i == half // 2))
            def _():
                open_head(h + 2)
                lead(h + 2)
                send_rims(h + 2)

            @pl.when(more)
            def _():
                turn(h + 1, (h + 1) % 2, 2 * i)
                turn(h + 1, (h + 1) % 2, 2 * i + 1)

            @pl.when(more & (i == half - 1))
            def _():
                assemble(h + 1)

            b = 2 * i
            ends = i == half - 1
            h_next = jnp.where(ends, ahead, h)
            b_next = jnp.where(ends, 0, b + 2)
            scores(h_next, b_next, 0)
            softmax(b + 1, 1)
            products(h, b, 0)
            scores(h_next, b_next + 1, 1)
            softmax(b_next, 0)
            products(h, b + 1, 1)
            return carry

        lax.fori_loop(0, half, pair, 0)
        deliver(h)
        return carry

    lax.fori_loop(0, heads, head, 0)
    near(hub_back, heads - 1)
    if heads > 1:
        finish(heads - 2)
    far(hub_back, heads - 1)
    finish(heads - 1)

    def close(h, carry):
        for copy in stores(h):
            copy.wait()

        @pl.when(me < last)
        def _():
            for copy in rims(h, True):
                copy.wait_send()
            backs(h, True).wait_send()
            for i in range(2):
                hop(hub_in, h, True, i).wait_send()
            for i in range(2):
                hop(hub_back, h, True, i).wait_send()

        @pl.when(me > 0)
        def _():
            for copy in rims(h, False):
                copy.wait_send()
            backs(h, False).wait_send()
            for i in range(2):
                hop(hub_in, h, False, i).wait_send()
            for i in range(2):
                hop(hub_back, h, False, i).wait_send()

        return carry

    lax.fori_loop(0, heads, close, 0)


def write_kernel(*refs):
    held, come, go = refs[8:]
    rows = refs[0].shape[0] // PARTS

    def pair(i, j):
        part = pl.ds(j * rows, rows)
        return (
            pltpu.make_async_copy(refs[i].at[part], held.at[i, part], come.at[i, j]),
            pltpu.make_async_copy(held.at[i, part], refs[4 + i].at[part], go.at[i, j]),
        )

    pairs = [pair(i, j) for i in range(4) for j in range(PARTS)]
    for load, _ in pairs:
        load.start()
    for load, store in pairs:
        load.wait()
        store.start()
    for _, store in pairs:
        store.wait()


def local(query_rows, key_rows, value_rows, out_grad, hub_blocks, local_lists):
    tokens, columns = query_rows.shape
    heads = columns // DH
    store = tokens + 2 * RIM + G * BLK
    blocks = tokens // BLK
    big = jax.ShapeDtypeStruct(query_rows.shape, BF)
    anywhere = pl.BlockSpec(memory_space=pl.ANY)
    smem = pl.BlockSpec(memory_space=pltpu.SMEM)
    vmem = pltpu.VMEM
    hub_shape = vmem((heads, 2, G * BLK, DH), BF)
    rim_shape = vmem((heads, 2, RIM, DH), BF)
    dma = pltpu.SemaphoreType.DMA
    units = 6 * heads * blocks * NE
    results = pl.pallas_call(
        layer_kernel,
        out_shape=[big] * 4,
        in_specs=[smem] * 2 + [anywhere] * 6,
        out_specs=[anywhere] * 4,
        scratch_shapes=[vmem((heads, store, DH), BF)] * 2
        + [vmem((heads, tokens, DH), BF)] * 2
        + [vmem((blocks, BLK, columns), BF)] * 2
        + [vmem((2, DH, store), BF)] * 2
        + [vmem((2, blocks, DH, BLK), BF)] * 2
        + [vmem((store, DH), F32)] * 2
        + [pltpu.SMEM((blocks, 8), F32)]
        + [vmem((heads, tokens, DH), BF)] * 4
        + [hub_shape] * 10
        + [vmem((2, G * BLK, DH), F32)]
        + [rim_shape] * 4
        + [vmem((NE * BLK, BLK), F32)] * 4
        + [vmem((8, BLK), F32)] * 2
        + [vmem((NE * BLK, BLK), BF)] * 4
        + [dma((2,)), dma((4, heads)), dma((4, heads))]
        + [dma((2, 2, heads))] * 4
        + [dma((2, heads))] * 2
        + [dma((2, 2, heads))] * 2,
        compiler_params=pltpu.CompilerParams(
            collective_id=0, has_side_effects=True, vmem_limit_bytes=56 << 20
        ),
        cost_estimate=pl.CostEstimate(
            flops=units * 2 * BLK * BLK * DH,
            bytes_accessed=16 * tokens * columns,
            transcendentals=heads * blocks * NE * BLK * BLK,
        ),
        name="layer",
    )(
        hub_blocks, local_lists.T, query_rows, key_rows, value_rows, out_grad,
        key_rows.reshape(blocks, BLK, columns), value_rows.reshape(blocks, BLK, columns),
    )
    return pl.pallas_call(
        write_kernel,
        out_shape=[big] * 4,
        in_specs=[anywhere] * 4,
        out_specs=[anywhere] * 4,
        scratch_shapes=[vmem((4, tokens, columns), BF), dma((4, PARTS)), dma((4, PARTS))],
        compiler_params=pltpu.CompilerParams(vmem_limit_bytes=60 << 20),
        name="write",
    )(*results)


def solution(mesh):
    spec = P("ctx", "head")
    return jax.shard_map(
        local,
        mesh=mesh,
        in_specs=(spec, spec, spec, spec, P(), P()),
        out_specs=(spec, spec, spec, spec),
        check_vma=False,
    )
```

```python
import functools
import math

import jax
import jax.numpy as jnp
from jax import lax
from jax.experimental import pallas as pl
from jax.experimental.pallas import tpu as pltpu
from jax.sharding import PartitionSpec as P

DH = 128
BLK = 128
HB = 3
G = 2
WIN = 2 * HB + 1
NE = WIN + G
RIM = HB * BLK
DEAD = -1e30
PARTS = 1
IN_AT, IN_GAP = 4, 7
BACK_AT, BACK_GAP, BACK_END = 3, 4, 12
SCALE = 1.0 / math.sqrt(DH)
C = SCALE * math.log2(math.e)
F32 = jnp.float32
BF = jnp.bfloat16
MESH = pl.DeviceIdType.MESH
ENTRY = [slice(e * BLK, (e + 1) * BLK) for e in range(NE)]


def dot(a, b):
    return jnp.dot(a, b, preferred_element_type=F32)


def fold(x, op):
    return op(x.reshape(x.shape[0] // 8, 8, x.shape[1]), axis=0)


def rows_of(b, n=1):
    return pl.ds(pl.multiple_of(b * BLK, BLK), n * BLK)


def cols_of(h):
    return pl.ds(pl.multiple_of(h * DH, DH), DH)


def layer_kernel(
    hub_ref, lists_ref, q_ref, k_ref, v_ref, g_ref, k3_ref, v3_ref, att_out, dq_out, dk_out, dv_out,
    kx, vx, qx, gx, ko, vo, kt, vt, qt, gt, dka, dva, bias, att, dq, dk, dv,
    hub_own, hub_fl, hub_fr, hub_tr, hub_tl,
    hg_own, hg_fl, hg_fr, hg_tr, hg_tl, hub_sum,
    rim_tl, rim_tr, rim_fl, rim_fr,
    s0, s1, p0, p1, m0, m1, w0, w1, l0, l1,
    whole_sem, load_sem, store_sem, rim_send, rim_recv, hub_send, hub_recv,
    back_send, back_recv, hg_send, hg_recv,
):
    heads, tokens, _ = qx.shape
    blocks = tokens // BLK
    extended = blocks + 2 * HB
    half = blocks // 2
    me = lax.axis_index("ctx")
    last = lax.axis_size("ctx") - 1
    own = pl.ds(RIM, tokens)
    hubs = slice(extended * BLK, (extended + G) * BLK)
    right_rim = slice((HB + blocks) * BLK, extended * BLK)
    S, PU, M, W, L = (s0, s1), (p0, p1), (m0, m1), (w0, w1), (l0, l1)

    def loads(h):
        pairs = (
            (k_ref, kx.at[h, own]), (v_ref, vx.at[h, own]),
            (q_ref, qx.at[h]), (g_ref, gx.at[h]),
        )
        return [
            pltpu.make_async_copy(src.at[:, cols_of(h)], dst, load_sem.at[i, h])
            for i, (src, dst) in enumerate(pairs)
        ]

    def wholes():
        return [
            pltpu.make_async_copy(src, dst, whole_sem.at[i])
            for i, (src, dst) in enumerate(((k3_ref, ko), (v3_ref, vo)))
        ]

    def stores(h, which=range(4)):
        pairs = ((att, att_out), (dq, dq_out), (dk, dk_out), (dv, dv_out))
        return [
            pltpu.make_async_copy(src.at[h], dst.at[:, cols_of(h)], store_sem.at[i, h])
            for i, (src, dst) in enumerate(pairs)
            if i in which
        ]

    def remote(src, dst, send, recv, to):
        return pltpu.make_async_remote_copy(
            src_ref=src, dst_ref=dst, send_sem=send, recv_sem=recv,
            device_id={"ctx": to}, device_id_type=MESH,
        )

    def rims(h, right):
        source = pl.ds(blocks * BLK, RIM) if right else pl.ds(RIM, RIM)
        target = pl.ds(0, RIM) if right else right_rim
        d = 0 if right else 1
        to = me + 1 if right else me - 1
        return [
            remote(x.at[h, source], x.at[h, target], rim_send.at[d, i, h], rim_recv.at[d, i, h], to)
            for i, x in enumerate((kx, vx))
        ]

    def backs(h, right):
        if right:
            return remote(rim_tr.at[h], rim_fl.at[h], back_send.at[0, h], back_recv.at[0, h], me + 1)
        return remote(rim_tl.at[h], rim_fr.at[h], back_send.at[1, h], back_recv.at[1, h], me - 1)

    hub_in = (hub_own, hub_fl, hub_fr, hub_tr, hub_tl, hub_send, hub_recv)
    hub_back = (hg_own, hg_fl, hg_fr, hg_tr, hg_tl, hg_send, hg_recv)

    def hop(chain, h, right, i, source=None):
        mine, fl, fr, tr, tl, send, recv = chain
        d = 0 if right else 1
        land, to = (fl, me + 1) if right else (fr, me - 1)
        if source is None:
            source = tr if right else tl
        return remote(source.at[h, i], land.at[h, i], send.at[d, i, h], recv.at[d, i, h], to)

    def step(chain, h, right):
        mine, fl, fr, tr, tl = chain[:5]
        first, final = (0, last) if right else (last, 0)
        got, sent = (fl, tr) if right else (fr, tl)
        for i in range(2):
            @pl.when(me == first)
            def _():
                hop(chain, h, right, i, mine).start()

            @pl.when(me != first)
            def _():
                hop(chain, h, right, i).wait_recv()

            @pl.when((me != first) & (me != final))
            def _():
                sent[h, i] = mine[h, i] + got[h, i]
                hop(chain, h, right, i).start()

    def both(chain, h, right, left):
        @pl.when(right)
        def _():
            step(chain, h, True)

        @pl.when(left)
        def _():
            step(chain, h, False)

    def near(chain, h):
        @pl.when(me <= last - me)
        def _():
            step(chain, h, True)

        @pl.when(me > last - me)
        def _():
            step(chain, h, False)

    def far(chain, h):
        @pl.when(me <= last - me)
        def _():
            step(chain, h, False)

        @pl.when(me > last - me)
        def _():
            step(chain, h, True)

    def chain_total(chain, h):
        mine, fl, fr = chain[:3]
        total = mine[h].astype(F32)
        total = total + jnp.where(me > 0, fl[h].astype(F32), 0.0)
        return total + jnp.where(me < last, fr[h].astype(F32), 0.0)

    def on_block(b):
        return [jnp.where(hub_ref[j] - me * blocks == b, 1.0, 0.0).astype(F32) for j in range(G)]

    def send_rims(h):
        @pl.when(me < last)
        def _():
            for copy in rims(h, True):
                copy.start()

        @pl.when(me > 0)
        def _():
            for copy in rims(h, False):
                copy.start()

    def pick():
        for j in range(G):
            spot = hub_ref[j] - me * blocks
            here = jnp.where((spot >= 0) & (spot < blocks), 1.0, 0.0).astype(F32)
            at = jnp.clip(spot, 0, blocks - 1)
            for i, x in enumerate((ko, vo)):
                block = (x[at].astype(F32) * here).astype(BF)
                for h in range(heads):
                    hub_own[h, i, ENTRY[j], :] = block[:, h * DH : (h + 1) * DH]

    def turn(h, slot, b):
        r = rows_of(b)
        e = rows_of(HB + b)
        qt[slot, b] = qx[h, r, :].T
        gt[slot, b] = gx[h, r, :].T
        kt[slot, :, e] = kx[h, e, :].T
        vt[slot, :, e] = vx[h, e, :].T

    def assemble(h):
        @pl.when(me > 0)
        def _():
            for copy in rims(h, True):
                copy.wait_recv()

        @pl.when(me == 0)
        def _():
            kx[h, 0:RIM, :] = jnp.zeros((RIM, DH), BF)
            vx[h, 0:RIM, :] = jnp.zeros((RIM, DH), BF)

        @pl.when(me < last)
        def _():
            for copy in rims(h, False):
                copy.wait_recv()

        @pl.when(me == last)
        def _():
            kx[h, right_rim, :] = jnp.zeros((RIM, DH), BF)
            vx[h, right_rim, :] = jnp.zeros((RIM, DH), BF)

        mine, fl, fr = hub_in[:3]
        for i, x in enumerate((kx, vx)):
            total = mine[h, i]
            total = total + jnp.where(me > 0, fl[h, i], jnp.zeros_like(total))
            total = total + jnp.where(me < last, fr[h, i], jnp.zeros_like(total))
            x[h, hubs, :] = total
        slot = h % 2
        for x, t in ((kx, kt), (vx, vt)):
            for e in list(range(HB)) + list(range(HB + blocks, extended + G)):
                es = slice(e * BLK, (e + 1) * BLK)
                t[slot, :, es] = x[h, es, :].T

    def scores(h, b, n):
        slot = h % 2
        qt_b, gt_b = qt[slot, b], gt[slot, b]
        window = rows_of(b, WIN)
        s_local = dot(kx[h, window, :], qt_b)
        s_hub = dot(kx[h, hubs, :], qt_b)
        S[n][: WIN * BLK, :] = s_local
        S[n][WIN * BLK :, :] = s_hub
        PU[n][: WIN * BLK, :] = dot(vx[h, window, :], gt_b)
        PU[n][WIN * BLK :, :] = dot(vx[h, hubs, :], gt_b)
        tops = [fold(s_local[ENTRY[e]], jnp.max) * C + bias[b, e] for e in range(WIN)]
        tops += [fold(s_hub[ENTRY[e]], jnp.max) * C for e in range(G)]
        M[n][...] = functools.reduce(jnp.maximum, tops)

    def softmax(b, n):
        shift = [bias[b, e] for e in range(WIN)] + [0.0] * G
        top = jnp.max(M[n][...], axis=0, keepdims=True)
        ps = [jnp.exp2(S[n][ENTRY[e], :] * C + (shift[e] - top)) for e in range(NE)]
        total = functools.reduce(jnp.add, [fold(p, jnp.sum) for p in ps])
        moved = functools.reduce(
            jnp.add, [fold(ps[e] * PU[n][ENTRY[e], :], jnp.sum) for e in range(NE)]
        )
        inverse = 1.0 / jnp.sum(total, axis=0, keepdims=True)
        offset = jnp.sum(moved, axis=0, keepdims=True) * inverse
        for e in range(NE):
            chances = ps[e] * inverse
            W[n][ENTRY[e], :] = chances.astype(BF)
            L[n][ENTRY[e], :] = (chances * (PU[n][ENTRY[e], :] - offset)).astype(BF)

    def products(h, b, n):
        slot = h % 2
        r = rows_of(b)
        window = rows_of(b, WIN)
        local = slice(0, WIN * BLK)
        hub = slice(WIN * BLK, NE * BLK)
        mixed = dot(vt[slot, :, window], W[n][local, :]) + dot(vt[slot, :, hubs], W[n][hub, :])
        att[h, r, :] = mixed.T.astype(BF)
        grad = dot(kt[slot, :, window], L[n][local, :]) + dot(kt[slot, :, hubs], L[n][hub, :])
        dq[h, r, :] = (grad * SCALE).T.astype(BF)
        a = dot(L[n][...], qx[h, r, :])
        d = dot(W[n][...], gx[h, r, :])
        dka[window, :] += a[local]
        dka[hubs, :] += a[hub]
        dva[window, :] += d[local]
        dva[hubs, :] += d[hub]

    def clear():
        dka[...] = jnp.zeros(dka.shape, F32)
        dva[...] = jnp.zeros(dva.shape, F32)

    def deliver(h):
        for i, (acc, scale) in enumerate(((dka, SCALE), (dva, 1.0))):
            rim_tl[h, i] = (acc[0:RIM, :] * scale).astype(BF)
            rim_tr[h, i] = (acc[right_rim, :] * scale).astype(BF)
            hg_own[h, i] = (acc[hubs, :] * scale).astype(BF)
        both(hub_back, h, me == 0, me == last)

        @pl.when(me < last)
        def _():
            backs(h, True).start()

        @pl.when(me > 0)
        def _():
            backs(h, False).start()

        def keep(b, carry):
            dk[h, rows_of(b), :] = (dka[rows_of(HB + b), :] * SCALE).astype(BF)
            dv[h, rows_of(b), :] = dva[rows_of(HB + b), :].astype(BF)
            return carry

        lax.fori_loop(0, blocks, keep, 0)
        clear()
        for copy in stores(h, (0, 1)):
            copy.start()

    def finish(h):
        @pl.when(me > 0)
        def _():
            backs(h, True).wait_recv()
            for i, x in enumerate((dk, dv)):
                x[h, 0:RIM, :] = (x[h, 0:RIM, :].astype(F32) + rim_fl[h, i].astype(F32)).astype(BF)

        @pl.when(me < last)
        def _():
            backs(h, False).wait_recv()
            end = slice(tokens - RIM, tokens)
            for i, x in enumerate((dk, dv)):
                x[h, end, :] = (x[h, end, :].astype(F32) + rim_fr[h, i].astype(F32)).astype(BF)

        hub_sum[...] = chain_total(hub_back, h)

        def add(b, carry):
            ons = on_block(b)
            for i, x in enumerate((dk, dv)):
                out = x[h, rows_of(b), :].astype(F32)
                for j in range(G):
                    out = out + ons[j] * hub_sum[i, ENTRY[j], :]
                x[h, rows_of(b), :] = out.astype(BF)
            return carry

        lax.fori_loop(0, blocks, add, 0)
        for copy in stores(h, (2, 3)):
            copy.start()

    def table(b, carry):
        listed = lists_ref.shape[0]
        at = me * blocks + b
        for e in range(WIN):
            r = e - HB
            count = jnp.int32(0)
            for j in range(listed):
                count = count + jnp.where(lists_ref[j, at] == r, 1, 0)
            alive = (at + r >= 0) & (at + r < blocks * (last + 1))
            value = jnp.float32(DEAD)
            for n in range(1, listed + 1):
                value = jnp.where(alive & (count == n), jnp.float32(math.log2(n)), value)
            bias[b, e] = value
        return carry

    barrier = pltpu.get_barrier_semaphore()

    @pl.when(me > 0)
    def _():
        pl.semaphore_signal(barrier, inc=1, device_id={"ctx": me - 1}, device_id_type=MESH)

    @pl.when(me < last)
    def _():
        pl.semaphore_signal(barrier, inc=1, device_id={"ctx": me + 1}, device_id_type=MESH)

    for copy in wholes():
        copy.start()

    def load_all(h, carry):
        for copy in loads(h):
            copy.start()
        return carry

    lax.fori_loop(0, heads, load_all, 0)

    @pl.when((me > 0) & (me < last))
    def _():
        pl.semaphore_wait(barrier, 2)

    @pl.when((me == 0) | (me == last))
    def _():
        pl.semaphore_wait(barrier, 1)

    def open_head(h):
        for copy in loads(h):
            copy.wait()

    def when_in(d):
        return jnp.where(d > 0, jnp.minimum(IN_AT + IN_GAP * (d - 1), 2 * half - 2), 0)

    def when_back(d):
        return jnp.where(d > 0, jnp.minimum(BACK_AT + BACK_GAP * (d - 1), BACK_END), -1)

    in_right, in_left = when_in(me), when_in(last - me)
    back_right, back_left = when_back(me), when_back(last - me)

    for copy in wholes():
        copy.wait()
    pick()
    near(hub_in, 0)
    open_head(0)
    send_rims(0)
    if heads > 1:
        both(hub_in, 1, me == 0, me == last)
    lax.fori_loop(0, blocks, table, 0)

    def turn_first(b, carry):
        turn(0, 0, b)
        return carry

    lax.fori_loop(0, blocks, turn_first, 0)
    far(hub_in, 0)
    if heads > 1:
        open_head(1)
        send_rims(1)
    clear()
    assemble(0)
    scores(0, 0, 0)
    softmax(0, 0)
    scores(0, 1, 1)

    def head(h, carry):
        more = h + 1 < heads
        ahead = jnp.minimum(h + 1, heads - 1)

        def pair(i, carry):
            two = h + 2 < heads
            opening = more & (h == 0) & (i == 0)
            both(hub_in, h + 1, opening & (me > 0) & (in_right < half), opening & (me < last) & (in_left < half))
            both(hub_in, h + 2, two & (i == in_right), two & (i == in_left))
            late = i + half
            both(hub_in, h + 1, more & (late == in_right), more & (late == in_left))
            both(hub_back, h - 1, (h > 0) & (i == back_right), (h > 0) & (i == back_left))
            both(hub_back, h - 2, (h > 1) & (late == back_right), (h > 1) & (late == back_left))

            @pl.when((h > 1) & (i == half - 3))
            def _():
                finish(h - 2)

            @pl.when((h + 2 < heads) & (i == half // 2))
            def _():
                open_head(h + 2)
                send_rims(h + 2)

            @pl.when(more)
            def _():
                turn(h + 1, (h + 1) % 2, 2 * i)
                turn(h + 1, (h + 1) % 2, 2 * i + 1)

            @pl.when(more & (i == half - 1))
            def _():
                assemble(h + 1)

            b = 2 * i
            ends = i == half - 1
            h_next = jnp.where(ends, ahead, h)
            b_next = jnp.where(ends, 0, b + 2)
            scores(h_next, b_next, 0)
            softmax(b + 1, 1)
            products(h, b, 0)
            scores(h_next, b_next + 1, 1)
            softmax(b_next, 0)
            products(h, b + 1, 1)
            return carry

        lax.fori_loop(0, half, pair, 0)
        deliver(h)
        return carry

    lax.fori_loop(0, heads, head, 0)
    both(hub_back, heads - 1, (me > 0) & (me <= last - me), (me < last) & (me > last - me))
    if heads > 1:
        both(hub_back, heads - 2, back_right >= half, back_left >= half)
        finish(heads - 2)
    far(hub_back, heads - 1)
    finish(heads - 1)

    def close(h, carry):
        for copy in stores(h):
            copy.wait()

        @pl.when(me < last)
        def _():
            for copy in rims(h, True):
                copy.wait_send()
            backs(h, True).wait_send()
            for i in range(2):
                hop(hub_in, h, True, i).wait_send()
            for i in range(2):
                hop(hub_back, h, True, i).wait_send()

        @pl.when(me > 0)
        def _():
            for copy in rims(h, False):
                copy.wait_send()
            backs(h, False).wait_send()
            for i in range(2):
                hop(hub_in, h, False, i).wait_send()
            for i in range(2):
                hop(hub_back, h, False, i).wait_send()

        return carry

    lax.fori_loop(0, heads, close, 0)


def write_kernel(*refs):
    held, come, go = refs[8:]
    rows = refs[0].shape[0] // PARTS

    def pair(i, j):
        part = pl.ds(j * rows, rows)
        return (
            pltpu.make_async_copy(refs[i].at[part], held.at[i, part], come.at[i, j]),
            pltpu.make_async_copy(held.at[i, part], refs[4 + i].at[part], go.at[i, j]),
        )

    pairs = [pair(i, j) for i in range(4) for j in range(PARTS)]
    for load, _ in pairs:
        load.start()
    for load, store in pairs:
        load.wait()
        store.start()
    for _, store in pairs:
        store.wait()


def local(query_rows, key_rows, value_rows, out_grad, hub_blocks, local_lists):
    tokens, columns = query_rows.shape
    heads = columns // DH
    store = tokens + 2 * RIM + G * BLK
    blocks = tokens // BLK
    big = jax.ShapeDtypeStruct(query_rows.shape, BF)
    anywhere = pl.BlockSpec(memory_space=pl.ANY)
    smem = pl.BlockSpec(memory_space=pltpu.SMEM)
    vmem = pltpu.VMEM
    hub_shape = vmem((heads, 2, G * BLK, DH), BF)
    rim_shape = vmem((heads, 2, RIM, DH), BF)
    dma = pltpu.SemaphoreType.DMA
    units = 6 * heads * blocks * NE
    results = pl.pallas_call(
        layer_kernel,
        out_shape=[big] * 4,
        in_specs=[smem] * 2 + [anywhere] * 6,
        out_specs=[anywhere] * 4,
        scratch_shapes=[vmem((heads, store, DH), BF)] * 2
        + [vmem((heads, tokens, DH), BF)] * 2
        + [vmem((blocks, BLK, columns), BF)] * 2
        + [vmem((2, DH, store), BF)] * 2
        + [vmem((2, blocks, DH, BLK), BF)] * 2
        + [vmem((store, DH), F32)] * 2
        + [pltpu.SMEM((blocks, 8), F32)]
        + [vmem((heads, tokens, DH), BF)] * 4
        + [hub_shape] * 10
        + [vmem((2, G * BLK, DH), F32)]
        + [rim_shape] * 4
        + [vmem((NE * BLK, BLK), F32)] * 4
        + [vmem((8, BLK), F32)] * 2
        + [vmem((NE * BLK, BLK), BF)] * 4
        + [dma((2,)), dma((4, heads)), dma((4, heads))]
        + [dma((2, 2, heads))] * 4
        + [dma((2, heads))] * 2
        + [dma((2, 2, heads))] * 2,
        compiler_params=pltpu.CompilerParams(
            collective_id=0, has_side_effects=True, vmem_limit_bytes=56 << 20
        ),
        cost_estimate=pl.CostEstimate(
            flops=units * 2 * BLK * BLK * DH,
            bytes_accessed=16 * tokens * columns,
            transcendentals=heads * blocks * NE * BLK * BLK,
        ),
        name="layer",
    )(
        hub_blocks, local_lists.T, query_rows, key_rows, value_rows, out_grad,
        key_rows.reshape(blocks, BLK, columns), value_rows.reshape(blocks, BLK, columns),
    )
    return pl.pallas_call(
        write_kernel,
        out_shape=[big] * 4,
        in_specs=[anywhere] * 4,
        out_specs=[anywhere] * 4,
        scratch_shapes=[vmem((4, tokens, columns), BF), dma((4, PARTS)), dma((4, PARTS))],
        compiler_params=pltpu.CompilerParams(vmem_limit_bytes=60 << 20),
        name="write",
    )(*results)


def solution(mesh):
    spec = P("ctx", "head")
    return jax.shard_map(
        local,
        mesh=mesh,
        in_specs=(spec, spec, spec, spec, P(), P()),
        out_specs=(spec, spec, spec, spec),
        check_vma=False,
    )
```

```python
import functools
import math

import jax
import jax.numpy as jnp
from jax import lax
from jax.experimental import pallas as pl
from jax.experimental.pallas import tpu as pltpu
from jax.sharding import PartitionSpec as P

DH = 128
BLK = 128
HB = 3
G = 2
WIN = 2 * HB + 1
NE = WIN + G
RIM = HB * BLK
DEAD = -1e30
PARTS = 1
IN_AT, IN_GAP = 6, 5
BACK_AT, BACK_GAP, BACK_END = 3, 4, 12
SCALE = 1.0 / math.sqrt(DH)
C = SCALE * math.log2(math.e)
F32 = jnp.float32
BF = jnp.bfloat16
MESH = pl.DeviceIdType.MESH
ENTRY = [slice(e * BLK, (e + 1) * BLK) for e in range(NE)]


def dot(a, b):
    return jnp.dot(a, b, preferred_element_type=F32)


def fold(x, op):
    return op(x.reshape(x.shape[0] // 8, 8, x.shape[1]), axis=0)


def rows_of(b, n=1):
    return pl.ds(pl.multiple_of(b * BLK, BLK), n * BLK)


def cols_of(h):
    return pl.ds(pl.multiple_of(h * DH, DH), DH)


def layer_kernel(
    hub_ref, lists_ref, q_ref, k_ref, v_ref, g_ref, k3_ref, v3_ref, att_out, dq_out, dk_out, dv_out,
    kx, vx, qx, gx, ko, vo, kt, vt, qt, gt, dka, dva, bias, att, dq, dk, dv,
    hub_own, hub_fl, hub_fr, hub_tr, hub_tl,
    hg_own, hg_fl, hg_fr, hg_tr, hg_tl, hub_sum,
    rim_tl, rim_tr, rim_fl, rim_fr,
    s0, s1, p0, p1, m0, m1, W, L,
    whole_sem, load_sem, store_sem, rim_send, rim_recv, hub_send, hub_recv,
    back_send, back_recv, hg_send, hg_recv,
):
    heads, tokens, _ = qx.shape
    blocks = tokens // BLK
    extended = blocks + 2 * HB
    half = blocks // 2
    me = lax.axis_index("ctx")
    last = lax.axis_size("ctx") - 1
    own = pl.ds(RIM, tokens)
    hubs = slice(extended * BLK, (extended + G) * BLK)
    right_rim = slice((HB + blocks) * BLK, extended * BLK)
    S, PU, M = (s0, s1), (p0, p1), (m0, m1)

    def loads(h):
        pairs = (
            (k_ref, kx.at[h, own]), (v_ref, vx.at[h, own]),
            (q_ref, qx.at[h]), (g_ref, gx.at[h]),
        )
        return [
            pltpu.make_async_copy(src.at[:, cols_of(h)], dst, load_sem.at[i, h])
            for i, (src, dst) in enumerate(pairs)
        ]

    def wholes():
        return [
            pltpu.make_async_copy(src, dst, whole_sem.at[i])
            for i, (src, dst) in enumerate(((k3_ref, ko), (v3_ref, vo)))
        ]

    def stores(h, which=range(4)):
        pairs = ((att, att_out), (dq, dq_out), (dk, dk_out), (dv, dv_out))
        return [
            pltpu.make_async_copy(src.at[h], dst.at[:, cols_of(h)], store_sem.at[i, h])
            for i, (src, dst) in enumerate(pairs)
            if i in which
        ]

    def remote(src, dst, send, recv, to):
        return pltpu.make_async_remote_copy(
            src_ref=src, dst_ref=dst, send_sem=send, recv_sem=recv,
            device_id={"ctx": to}, device_id_type=MESH,
        )

    def rims(h, right):
        source = pl.ds(blocks * BLK, RIM) if right else pl.ds(RIM, RIM)
        target = pl.ds(0, RIM) if right else right_rim
        d = 0 if right else 1
        to = me + 1 if right else me - 1
        return [
            remote(x.at[h, source], x.at[h, target], rim_send.at[d, i, h], rim_recv.at[d, i, h], to)
            for i, x in enumerate((kx, vx))
        ]

    def backs(h, right):
        if right:
            return remote(rim_tr.at[h], rim_fl.at[h], back_send.at[0, h], back_recv.at[0, h], me + 1)
        return remote(rim_tl.at[h], rim_fr.at[h], back_send.at[1, h], back_recv.at[1, h], me - 1)

    hub_in = (hub_own, hub_fl, hub_fr, hub_tr, hub_tl, hub_send, hub_recv)
    hub_back = (hg_own, hg_fl, hg_fr, hg_tr, hg_tl, hg_send, hg_recv)

    def hop(chain, h, right, i, source=None):
        mine, fl, fr, tr, tl, send, recv = chain
        d = 0 if right else 1
        land, to = (fl, me + 1) if right else (fr, me - 1)
        if source is None:
            source = tr if right else tl
        return remote(source.at[h, i], land.at[h, i], send.at[d, i, h], recv.at[d, i, h], to)

    def step(chain, h, right):
        mine, fl, fr, tr, tl = chain[:5]
        first, final = (0, last) if right else (last, 0)
        got, sent = (fl, tr) if right else (fr, tl)
        for i in range(2):
            @pl.when(me == first)
            def _():
                hop(chain, h, right, i, mine).start()

            @pl.when(me != first)
            def _():
                hop(chain, h, right, i).wait_recv()

            @pl.when((me != first) & (me != final))
            def _():
                sent[h, i] = mine[h, i] + got[h, i]
                hop(chain, h, right, i).start()

    def both(chain, h, right, left):
        @pl.when(right)
        def _():
            step(chain, h, True)

        @pl.when(left)
        def _():
            step(chain, h, False)

    def near(chain, h):
        @pl.when(me <= last - me)
        def _():
            step(chain, h, True)

        @pl.when(me > last - me)
        def _():
            step(chain, h, False)

    def far(chain, h):
        @pl.when(me <= last - me)
        def _():
            step(chain, h, False)

        @pl.when(me > last - me)
        def _():
            step(chain, h, True)

    def chain_total(chain, h):
        mine, fl, fr = chain[:3]
        total = mine[h].astype(F32)
        total = total + jnp.where(me > 0, fl[h].astype(F32), 0.0)
        return total + jnp.where(me < last, fr[h].astype(F32), 0.0)

    def on_block(b):
        return [jnp.where(hub_ref[j] - me * blocks == b, 1.0, 0.0).astype(F32) for j in range(G)]

    def send_rims(h):
        @pl.when(me < last)
        def _():
            for copy in rims(h, True):
                copy.start()

        @pl.when(me > 0)
        def _():
            for copy in rims(h, False):
                copy.start()

    def pick():
        for j in range(G):
            spot = hub_ref[j] - me * blocks
            here = jnp.where((spot >= 0) & (spot < blocks), 1.0, 0.0).astype(F32)
            at = jnp.clip(spot, 0, blocks - 1)
            for i, x in enumerate((ko, vo)):
                block = (x[at].astype(F32) * here).astype(BF)
                for h in range(heads):
                    hub_own[h, i, ENTRY[j], :] = block[:, h * DH : (h + 1) * DH]

    def turn(h, slot, b):
        r = rows_of(b)
        e = rows_of(HB + b)
        qt[slot, b] = qx[h, r, :].T
        gt[slot, b] = gx[h, r, :].T
        kt[slot, :, e] = kx[h, e, :].T
        vt[slot, :, e] = vx[h, e, :].T

    def assemble(h):
        @pl.when(me > 0)
        def _():
            for copy in rims(h, True):
                copy.wait_recv()

        @pl.when(me == 0)
        def _():
            kx[h, 0:RIM, :] = jnp.zeros((RIM, DH), BF)
            vx[h, 0:RIM, :] = jnp.zeros((RIM, DH), BF)

        @pl.when(me < last)
        def _():
            for copy in rims(h, False):
                copy.wait_recv()

        @pl.when(me == last)
        def _():
            kx[h, right_rim, :] = jnp.zeros((RIM, DH), BF)
            vx[h, right_rim, :] = jnp.zeros((RIM, DH), BF)

        mine, fl, fr = hub_in[:3]
        for i, x in enumerate((kx, vx)):
            total = mine[h, i]
            total = total + jnp.where(me > 0, fl[h, i], jnp.zeros_like(total))
            total = total + jnp.where(me < last, fr[h, i], jnp.zeros_like(total))
            x[h, hubs, :] = total
        slot = h % 2
        for x, t in ((kx, kt), (vx, vt)):
            for e in list(range(HB)) + list(range(HB + blocks, extended + G)):
                es = slice(e * BLK, (e + 1) * BLK)
                t[slot, :, es] = x[h, es, :].T

    def scores(h, b, n):
        slot = h % 2
        qt_b, gt_b = qt[slot, b], gt[slot, b]
        window = rows_of(b, WIN)
        s_local = dot(kx[h, window, :], qt_b)
        s_hub = dot(kx[h, hubs, :], qt_b)
        S[n][: WIN * BLK, :] = s_local
        S[n][WIN * BLK :, :] = s_hub
        PU[n][: WIN * BLK, :] = dot(vx[h, window, :], gt_b)
        PU[n][WIN * BLK :, :] = dot(vx[h, hubs, :], gt_b)
        tops = [fold(s_local[ENTRY[e]], jnp.max) * C + bias[b, e] for e in range(WIN)]
        tops += [fold(s_hub[ENTRY[e]], jnp.max) * C for e in range(G)]
        M[n][...] = functools.reduce(jnp.maximum, tops)

    def softmax(b, n):
        shift = [bias[b, e] for e in range(WIN)] + [0.0] * G
        top = jnp.max(M[n][...], axis=0, keepdims=True)
        ps = [jnp.exp2(S[n][ENTRY[e], :] * C + (shift[e] - top)) for e in range(NE)]
        total = functools.reduce(jnp.add, [fold(p, jnp.sum) for p in ps])
        moved = functools.reduce(
            jnp.add, [fold(ps[e] * PU[n][ENTRY[e], :], jnp.sum) for e in range(NE)]
        )
        inverse = 1.0 / jnp.sum(total, axis=0, keepdims=True)
        offset = jnp.sum(moved, axis=0, keepdims=True) * inverse
        for e in range(NE):
            chances = ps[e] * inverse
            at = e + n if e < WIN else e + 1
            place = (slice(at * BLK, (at + 1) * BLK), slice(n * BLK, (n + 1) * BLK))
            W[place] = chances.astype(BF)
            L[place] = (chances * (PU[n][ENTRY[e], :] - offset)).astype(BF)

    def products(h, b):
        slot = h % 2
        r = rows_of(b, 2)
        window = rows_of(b, WIN + 1)
        local = slice(0, (WIN + 1) * BLK)
        hub = slice((WIN + 1) * BLK, (NE + 1) * BLK)
        mixed = dot(vt[slot, :, window], W[local, :]) + dot(vt[slot, :, hubs], W[hub, :])
        att[h, r, :] = mixed.T.astype(BF)
        grad = dot(kt[slot, :, window], L[local, :]) + dot(kt[slot, :, hubs], L[hub, :])
        dq[h, r, :] = (grad * SCALE).T.astype(BF)
        for n in range(2):
            lanes = slice(n * BLK, (n + 1) * BLK)
            mine = slice(n * BLK, (n + WIN) * BLK)
            q, g = qx[h, rows_of(b + n), :], gx[h, rows_of(b + n), :]
            dka[rows_of(b + n, WIN), :] += dot(L[mine, lanes], q)
            dka[hubs, :] += dot(L[hub, lanes], q)
            dva[rows_of(b + n, WIN), :] += dot(W[mine, lanes], g)
            dva[hubs, :] += dot(W[hub, lanes], g)

    def corners():
        for x in (W, L):
            x[0:BLK, BLK : 2 * BLK] = jnp.zeros((BLK, BLK), BF)
            x[WIN * BLK : (WIN + 1) * BLK, 0:BLK] = jnp.zeros((BLK, BLK), BF)

    def clear():
        dka[...] = jnp.zeros(dka.shape, F32)
        dva[...] = jnp.zeros(dva.shape, F32)

    def deliver(h):
        for i, (acc, scale) in enumerate(((dka, SCALE), (dva, 1.0))):
            rim_tl[h, i] = (acc[0:RIM, :] * scale).astype(BF)
            rim_tr[h, i] = (acc[right_rim, :] * scale).astype(BF)
            hg_own[h, i] = (acc[hubs, :] * scale).astype(BF)
        both(hub_back, h, me == 0, me == last)

        @pl.when(me < last)
        def _():
            backs(h, True).start()

        @pl.when(me > 0)
        def _():
            backs(h, False).start()

        def keep(b, carry):
            dk[h, rows_of(b), :] = (dka[rows_of(HB + b), :] * SCALE).astype(BF)
            dv[h, rows_of(b), :] = dva[rows_of(HB + b), :].astype(BF)
            return carry

        lax.fori_loop(0, blocks, keep, 0)
        clear()
        for copy in stores(h, (0, 1)):
            copy.start()

    def finish(h):
        @pl.when(me > 0)
        def _():
            backs(h, True).wait_recv()
            for i, x in enumerate((dk, dv)):
                x[h, 0:RIM, :] = (x[h, 0:RIM, :].astype(F32) + rim_fl[h, i].astype(F32)).astype(BF)

        @pl.when(me < last)
        def _():
            backs(h, False).wait_recv()
            end = slice(tokens - RIM, tokens)
            for i, x in enumerate((dk, dv)):
                x[h, end, :] = (x[h, end, :].astype(F32) + rim_fr[h, i].astype(F32)).astype(BF)

        hub_sum[...] = chain_total(hub_back, h)

        def add(b, carry):
            ons = on_block(b)
            for i, x in enumerate((dk, dv)):
                out = x[h, rows_of(b), :].astype(F32)
                for j in range(G):
                    out = out + ons[j] * hub_sum[i, ENTRY[j], :]
                x[h, rows_of(b), :] = out.astype(BF)
            return carry

        lax.fori_loop(0, blocks, add, 0)
        for copy in stores(h, (2, 3)):
            copy.start()

    def table(b, carry):
        listed = lists_ref.shape[0]
        at = me * blocks + b
        for e in range(WIN):
            r = e - HB
            count = jnp.int32(0)
            for j in range(listed):
                count = count + jnp.where(lists_ref[j, at] == r, 1, 0)
            alive = (at + r >= 0) & (at + r < blocks * (last + 1))
            value = jnp.float32(DEAD)
            for n in range(1, listed + 1):
                value = jnp.where(alive & (count == n), jnp.float32(math.log2(n)), value)
            bias[b, e] = value
        return carry

    barrier = pltpu.get_barrier_semaphore()

    @pl.when(me > 0)
    def _():
        pl.semaphore_signal(barrier, inc=1, device_id={"ctx": me - 1}, device_id_type=MESH)

    @pl.when(me < last)
    def _():
        pl.semaphore_signal(barrier, inc=1, device_id={"ctx": me + 1}, device_id_type=MESH)

    for copy in wholes():
        copy.start()

    def load_all(h, carry):
        for copy in loads(h):
            copy.start()
        return carry

    lax.fori_loop(0, heads, load_all, 0)

    @pl.when((me > 0) & (me < last))
    def _():
        pl.semaphore_wait(barrier, 2)

    @pl.when((me == 0) | (me == last))
    def _():
        pl.semaphore_wait(barrier, 1)

    def open_head(h):
        for copy in loads(h):
            copy.wait()

    def when_in(d):
        return jnp.where(d > 0, jnp.minimum(IN_AT + IN_GAP * (d - 1), 2 * half - 1), 0)

    def when_back(d):
        return jnp.where(d > 0, jnp.minimum(BACK_AT + BACK_GAP * (d - 1), BACK_END), -1)

    in_right, in_left = when_in(me), when_in(last - me)
    back_right, back_left = when_back(me), when_back(last - me)

    for copy in wholes():
        copy.wait()
    pick()
    near(hub_in, 0)
    open_head(0)
    send_rims(0)
    if heads > 1:
        both(hub_in, 1, me == 0, me == last)
    lax.fori_loop(0, blocks, table, 0)

    def turn_first(b, carry):
        turn(0, 0, b)
        return carry

    inside = (me > 0) & (me < last)

    @pl.when(inside)
    def _():
        far(hub_in, 0)

    lax.fori_loop(0, blocks, turn_first, 0)

    @pl.when((me == 0) | (me == last))
    def _():
        far(hub_in, 0)

    if heads > 1:
        open_head(1)
        send_rims(1)
    clear()
    corners()
    assemble(0)
    scores(0, 0, 0)
    softmax(0, 0)
    scores(0, 1, 1)

    def head(h, carry):
        more = h + 1 < heads
        ahead = jnp.minimum(h + 1, heads - 1)

        def pair(i, carry):
            two = h + 2 < heads
            opening = more & (h == 0) & (i == 0)
            both(hub_in, h + 1, opening & (me > 0) & (in_right < half), opening & (me < last) & (in_left < half))
            both(hub_in, h + 2, two & (i == in_right), two & (i == in_left))
            late = i + half
            both(hub_in, h + 1, more & (late == in_right), more & (late == in_left))
            both(hub_back, h - 1, (h > 0) & (i == back_right), (h > 0) & (i == back_left))
            both(hub_back, h - 2, (h > 1) & (late == back_right), (h > 1) & (late == back_left))

            @pl.when((h > 1) & (i == half - 3))
            def _():
                finish(h - 2)

            @pl.when((h + 2 < heads) & (i == half // 2))
            def _():
                open_head(h + 2)
                send_rims(h + 2)

            @pl.when(more)
            def _():
                turn(h + 1, (h + 1) % 2, 2 * i)
                turn(h + 1, (h + 1) % 2, 2 * i + 1)

            @pl.when(more & (i == half - 1))
            def _():
                assemble(h + 1)

            b = 2 * i
            ends = i == half - 1
            h_next = jnp.where(ends, ahead, h)
            b_next = jnp.where(ends, 0, b + 2)
            scores(h_next, b_next, 0)
            softmax(b + 1, 1)
            products(h, b)
            scores(h_next, b_next + 1, 1)
            softmax(b_next, 0)
            return carry

        lax.fori_loop(0, half, pair, 0)
        deliver(h)
        return carry

    lax.fori_loop(0, heads, head, 0)
    both(hub_back, heads - 1, (me > 0) & (me <= last - me), (me < last) & (me > last - me))
    @pl.when(inside)
    def _():
        far(hub_back, heads - 1)

    if heads > 1:
        both(hub_back, heads - 2, back_right >= half, back_left >= half)
        finish(heads - 2)

    @pl.when((me == 0) | (me == last))
    def _():
        far(hub_back, heads - 1)

    finish(heads - 1)

    def close(h, carry):
        for copy in stores(h):
            copy.wait()

        @pl.when(me < last)
        def _():
            for copy in rims(h, True):
                copy.wait_send()
            backs(h, True).wait_send()
            for i in range(2):
                hop(hub_in, h, True, i).wait_send()
            for i in range(2):
                hop(hub_back, h, True, i).wait_send()

        @pl.when(me > 0)
        def _():
            for copy in rims(h, False):
                copy.wait_send()
            backs(h, False).wait_send()
            for i in range(2):
                hop(hub_in, h, False, i).wait_send()
            for i in range(2):
                hop(hub_back, h, False, i).wait_send()

        return carry

    lax.fori_loop(0, heads, close, 0)


def write_kernel(*refs):
    held, come, go = refs[8:]
    rows = refs[0].shape[0] // PARTS

    def pair(i, j):
        part = pl.ds(j * rows, rows)
        return (
            pltpu.make_async_copy(refs[i].at[part], held.at[i, part], come.at[i, j]),
            pltpu.make_async_copy(held.at[i, part], refs[4 + i].at[part], go.at[i, j]),
        )

    pairs = [pair(i, j) for i in range(4) for j in range(PARTS)]
    for load, _ in pairs:
        load.start()
    for load, store in pairs:
        load.wait()
        store.start()
    for _, store in pairs:
        store.wait()


def local(query_rows, key_rows, value_rows, out_grad, hub_blocks, local_lists):
    tokens, columns = query_rows.shape
    heads = columns // DH
    store = tokens + 2 * RIM + G * BLK
    blocks = tokens // BLK
    big = jax.ShapeDtypeStruct(query_rows.shape, BF)
    anywhere = pl.BlockSpec(memory_space=pl.ANY)
    smem = pl.BlockSpec(memory_space=pltpu.SMEM)
    vmem = pltpu.VMEM
    hub_shape = vmem((heads, 2, G * BLK, DH), BF)
    rim_shape = vmem((heads, 2, RIM, DH), BF)
    dma = pltpu.SemaphoreType.DMA
    units = 6 * heads * blocks * NE
    results = pl.pallas_call(
        layer_kernel,
        out_shape=[big] * 4,
        in_specs=[smem] * 2 + [anywhere] * 6,
        out_specs=[anywhere] * 4,
        scratch_shapes=[vmem((heads, store, DH), BF)] * 2
        + [vmem((heads, tokens, DH), BF)] * 2
        + [vmem((blocks, BLK, columns), BF)] * 2
        + [vmem((2, DH, store), BF)] * 2
        + [vmem((2, blocks, DH, BLK), BF)] * 2
        + [vmem((store, DH), F32)] * 2
        + [pltpu.SMEM((blocks, 8), F32)]
        + [vmem((heads, tokens, DH), BF)] * 4
        + [hub_shape] * 10
        + [vmem((2, G * BLK, DH), F32)]
        + [rim_shape] * 4
        + [vmem((NE * BLK, BLK), F32)] * 4
        + [vmem((8, BLK), F32)] * 2
        + [vmem(((NE + 1) * BLK, 2 * BLK), BF)] * 2
        + [dma((2,)), dma((4, heads)), dma((4, heads))]
        + [dma((2, 2, heads))] * 4
        + [dma((2, heads))] * 2
        + [dma((2, 2, heads))] * 2,
        compiler_params=pltpu.CompilerParams(
            collective_id=0, has_side_effects=True, vmem_limit_bytes=56 << 20
        ),
        cost_estimate=pl.CostEstimate(
            flops=units * 2 * BLK * BLK * DH,
            bytes_accessed=16 * tokens * columns,
            transcendentals=heads * blocks * NE * BLK * BLK,
        ),
        name="layer",
    )(
        hub_blocks, local_lists.T, query_rows, key_rows, value_rows, out_grad,
        key_rows.reshape(blocks, BLK, columns), value_rows.reshape(blocks, BLK, columns),
    )
    return pl.pallas_call(
        write_kernel,
        out_shape=[big] * 4,
        in_specs=[anywhere] * 4,
        out_specs=[anywhere] * 4,
        scratch_shapes=[vmem((4, tokens, columns), BF), dma((4, PARTS)), dma((4, PARTS))],
        compiler_params=pltpu.CompilerParams(vmem_limit_bytes=60 << 20),
        name="write",
    )(*results)


def solution(mesh):
    spec = P("ctx", "head")
    return jax.shard_map(
        local,
        mesh=mesh,
        in_specs=(spec, spec, spec, spec, P(), P()),
        out_specs=(spec, spec, spec, spec),
        check_vma=False,
    )
```

```python
import functools
import math

import jax
import jax.numpy as jnp
from jax import lax
from jax.experimental import pallas as pl
from jax.experimental.pallas import tpu as pltpu
from jax.sharding import PartitionSpec as P

DH = 128
BLK = 128
HB = 3
G = 2
WIN = 2 * HB + 1
NE = WIN + G
RIM = HB * BLK
DEAD = -1e30
PARTS = 1
IN_AT, IN_GAP = 6, 5
BACK_AT, BACK_GAP, BACK_END = 3, 4, 12
SCALE = 1.0 / math.sqrt(DH)
C = SCALE * math.log2(math.e)
F32 = jnp.float32
BF = jnp.bfloat16
MESH = pl.DeviceIdType.MESH
ENTRY = [slice(e * BLK, (e + 1) * BLK) for e in range(NE)]


def dot(a, b):
    return jnp.dot(a, b, preferred_element_type=F32)


def fold(x, op):
    return op(x.reshape(x.shape[0] // 8, 8, x.shape[1]), axis=0)


def rows_of(b, n=1):
    return pl.ds(pl.multiple_of(b * BLK, BLK), n * BLK)


def cols_of(h):
    return pl.ds(pl.multiple_of(h * DH, DH), DH)


def layer_kernel(
    hub_ref, lists_ref, q_ref, k_ref, v_ref, g_ref, k3_ref, v3_ref, att_out, dq_out, dk_out, dv_out,
    kx, vx, qx, gx, ko, vo, kt, vt, qt, gt, dka, dva, bias, att, dq, dk, dv,
    hub_own, hub_fl, hub_fr, hub_tr, hub_tl,
    hg_own, hg_fl, hg_fr, hg_tr, hg_tl, hub_sum,
    rim_tl, rim_tr, rim_fl, rim_fr,
    s0, s1, p0, p1, m0, m1, W, L,
    whole_sem, load_sem, store_sem, rim_send, rim_recv, hub_send, hub_recv,
    back_send, back_recv, hg_send, hg_recv,
):
    heads, tokens, _ = qx.shape
    blocks = tokens // BLK
    extended = blocks + 2 * HB
    half = blocks // 2
    me = lax.axis_index("ctx")
    last = lax.axis_size("ctx") - 1
    own = pl.ds(RIM, tokens)
    hubs = slice(extended * BLK, (extended + G) * BLK)
    right_rim = slice((HB + blocks) * BLK, extended * BLK)
    S, PU, M = (s0, s1), (p0, p1), (m0, m1)

    def loads(h):
        pairs = (
            (k_ref, kx.at[h, own]), (v_ref, vx.at[h, own]),
            (q_ref, qx.at[h]), (g_ref, gx.at[h]),
        )
        return [
            pltpu.make_async_copy(src.at[:, cols_of(h)], dst, load_sem.at[i, h])
            for i, (src, dst) in enumerate(pairs)
        ]

    def wholes():
        return [
            pltpu.make_async_copy(src, dst, whole_sem.at[i])
            for i, (src, dst) in enumerate(((k3_ref, ko), (v3_ref, vo)))
        ]

    def stores(h, which=range(4)):
        pairs = ((att, att_out), (dq, dq_out), (dk, dk_out), (dv, dv_out))
        return [
            pltpu.make_async_copy(src.at[h], dst.at[:, cols_of(h)], store_sem.at[i, h])
            for i, (src, dst) in enumerate(pairs)
            if i in which
        ]

    def remote(src, dst, send, recv, to):
        return pltpu.make_async_remote_copy(
            src_ref=src, dst_ref=dst, send_sem=send, recv_sem=recv,
            device_id={"ctx": to}, device_id_type=MESH,
        )

    def rims(h, right):
        source = pl.ds(blocks * BLK, RIM) if right else pl.ds(RIM, RIM)
        target = pl.ds(0, RIM) if right else right_rim
        d = 0 if right else 1
        to = me + 1 if right else me - 1
        return [
            remote(x.at[h, source], x.at[h, target], rim_send.at[d, i, h], rim_recv.at[d, i, h], to)
            for i, x in enumerate((kx, vx))
        ]

    def backs(h, right):
        if right:
            return remote(rim_tr.at[h], rim_fl.at[h], back_send.at[0, h], back_recv.at[0, h], me + 1)
        return remote(rim_tl.at[h], rim_fr.at[h], back_send.at[1, h], back_recv.at[1, h], me - 1)

    hub_in = (hub_own, hub_fl, hub_fr, hub_tr, hub_tl, hub_send, hub_recv)
    hub_back = (hg_own, hg_fl, hg_fr, hg_tr, hg_tl, hg_send, hg_recv)

    def hop(chain, h, right, i, source=None):
        mine, fl, fr, tr, tl, send, recv = chain
        d = 0 if right else 1
        land, to = (fl, me + 1) if right else (fr, me - 1)
        if source is None:
            source = tr if right else tl
        return remote(source.at[h, i], land.at[h, i], send.at[d, i, h], recv.at[d, i, h], to)

    def step(chain, h, right):
        mine, fl, fr, tr, tl = chain[:5]
        first, final = (0, last) if right else (last, 0)
        got, sent = (fl, tr) if right else (fr, tl)
        for i in range(2):
            @pl.when(me == first)
            def _():
                hop(chain, h, right, i, mine).start()

            @pl.when(me != first)
            def _():
                hop(chain, h, right, i).wait_recv()

            @pl.when((me != first) & (me != final))
            def _():
                sent[h, i] = mine[h, i] + got[h, i]
                hop(chain, h, right, i).start()

    def both(chain, h, right, left):
        @pl.when(right)
        def _():
            step(chain, h, True)

        @pl.when(left)
        def _():
            step(chain, h, False)

    def near(chain, h):
        @pl.when(me <= last - me)
        def _():
            step(chain, h, True)

        @pl.when(me > last - me)
        def _():
            step(chain, h, False)

    def far(chain, h):
        @pl.when(me <= last - me)
        def _():
            step(chain, h, False)

        @pl.when(me > last - me)
        def _():
            step(chain, h, True)

    def chain_total(chain, h):
        mine, fl, fr = chain[:3]
        total = mine[h].astype(F32)
        total = total + jnp.where(me > 0, fl[h].astype(F32), 0.0)
        return total + jnp.where(me < last, fr[h].astype(F32), 0.0)

    def on_block(b):
        return [jnp.where(hub_ref[j] - me * blocks == b, 1.0, 0.0).astype(F32) for j in range(G)]

    def send_rims(h):
        @pl.when(me < last)
        def _():
            for copy in rims(h, True):
                copy.start()

        @pl.when(me > 0)
        def _():
            for copy in rims(h, False):
                copy.start()

    def pick():
        for j in range(G):
            spot = hub_ref[j] - me * blocks
            here = jnp.where((spot >= 0) & (spot < blocks), 1.0, 0.0).astype(F32)
            at = jnp.clip(spot, 0, blocks - 1)
            for i, x in enumerate((ko, vo)):
                block = (x[at].astype(F32) * here).astype(BF)
                for h in range(heads):
                    hub_own[h, i, ENTRY[j], :] = block[:, h * DH : (h + 1) * DH]

    def turn(h, slot, b):
        r = rows_of(b)
        e = rows_of(HB + b)
        qt[slot, b] = qx[h, r, :].T
        gt[slot, b] = gx[h, r, :].T
        kt[slot, :, e] = kx[h, e, :].T
        vt[slot, :, e] = vx[h, e, :].T

    def assemble(h):
        @pl.when(me > 0)
        def _():
            for copy in rims(h, True):
                copy.wait_recv()

        @pl.when(me == 0)
        def _():
            kx[h, 0:RIM, :] = jnp.zeros((RIM, DH), BF)
            vx[h, 0:RIM, :] = jnp.zeros((RIM, DH), BF)

        @pl.when(me < last)
        def _():
            for copy in rims(h, False):
                copy.wait_recv()

        @pl.when(me == last)
        def _():
            kx[h, right_rim, :] = jnp.zeros((RIM, DH), BF)
            vx[h, right_rim, :] = jnp.zeros((RIM, DH), BF)

        mine, fl, fr = hub_in[:3]
        for i, x in enumerate((kx, vx)):
            total = mine[h, i]
            total = total + jnp.where(me > 0, fl[h, i], jnp.zeros_like(total))
            total = total + jnp.where(me < last, fr[h, i], jnp.zeros_like(total))
            x[h, hubs, :] = total
        slot = h % 2
        for x, t in ((kx, kt), (vx, vt)):
            for e in list(range(HB)) + list(range(HB + blocks, extended + G)):
                es = slice(e * BLK, (e + 1) * BLK)
                t[slot, :, es] = x[h, es, :].T

    def scores(h, b, n):
        slot = h % 2
        qt_b, gt_b = qt[slot, b], gt[slot, b]
        window = rows_of(b, WIN)
        s_local = dot(kx[h, window, :], qt_b)
        s_hub = dot(kx[h, hubs, :], qt_b)
        S[n][: WIN * BLK, :] = s_local
        S[n][WIN * BLK :, :] = s_hub
        PU[n][: WIN * BLK, :] = dot(vx[h, window, :], gt_b)
        PU[n][WIN * BLK :, :] = dot(vx[h, hubs, :], gt_b)
        tops = [fold(s_local[ENTRY[e]], jnp.max) * C + bias[b, e] for e in range(WIN)]
        tops += [fold(s_hub[ENTRY[e]], jnp.max) * C for e in range(G)]
        M[n][...] = functools.reduce(jnp.maximum, tops)

    def softmax(b, n):
        shift = [bias[b, e] for e in range(WIN)] + [0.0] * G
        top = jnp.max(M[n][...], axis=0, keepdims=True)
        ps = [jnp.exp2(S[n][ENTRY[e], :] * C + (shift[e] - top)) for e in range(NE)]
        total = functools.reduce(jnp.add, [fold(p, jnp.sum) for p in ps])
        moved = functools.reduce(
            jnp.add, [fold(ps[e] * PU[n][ENTRY[e], :], jnp.sum) for e in range(NE)]
        )
        inverse = 1.0 / jnp.sum(total, axis=0, keepdims=True)
        offset = jnp.sum(moved, axis=0, keepdims=True) * inverse
        for e in range(NE):
            chances = ps[e] * inverse
            at = e + n if e < WIN else e + 1
            place = (slice(at * BLK, (at + 1) * BLK), slice(n * BLK, (n + 1) * BLK))
            W[place] = chances.astype(BF)
            L[place] = (chances * (PU[n][ENTRY[e], :] - offset)).astype(BF)

    def products(h, b):
        slot = h % 2
        r = rows_of(b, 2)
        window = rows_of(b, WIN + 1)
        local = slice(0, (WIN + 1) * BLK)
        hub = slice((WIN + 1) * BLK, (NE + 1) * BLK)
        mixed = dot(vt[slot, :, window], W[local, :]) + dot(vt[slot, :, hubs], W[hub, :])
        att[h, r, :] = mixed.T.astype(BF)
        grad = dot(kt[slot, :, window], L[local, :]) + dot(kt[slot, :, hubs], L[hub, :])
        dq[h, r, :] = (grad * SCALE).T.astype(BF)
        for n in range(2):
            lanes = slice(n * BLK, (n + 1) * BLK)
            mine = slice(n * BLK, (n + WIN) * BLK)
            q, g = qx[h, rows_of(b + n), :], gx[h, rows_of(b + n), :]
            dka[rows_of(b + n, WIN), :] += dot(L[mine, lanes], q)
            dka[hubs, :] += dot(L[hub, lanes], q)
            dva[rows_of(b + n, WIN), :] += dot(W[mine, lanes], g)
            dva[hubs, :] += dot(W[hub, lanes], g)

    def corners():
        for x in (W, L):
            x[0:BLK, BLK : 2 * BLK] = jnp.zeros((BLK, BLK), BF)
            x[WIN * BLK : (WIN + 1) * BLK, 0:BLK] = jnp.zeros((BLK, BLK), BF)

    def clear():
        dka[...] = jnp.zeros(dka.shape, F32)
        dva[...] = jnp.zeros(dva.shape, F32)

    def deliver(h):
        for i, (acc, scale) in enumerate(((dka, SCALE), (dva, 1.0))):
            rim_tl[h, i] = (acc[0:RIM, :] * scale).astype(BF)
            rim_tr[h, i] = (acc[right_rim, :] * scale).astype(BF)
            hg_own[h, i] = (acc[hubs, :] * scale).astype(BF)
        both(hub_back, h, me == 0, me == last)

        @pl.when(me < last)
        def _():
            backs(h, True).start()

        @pl.when(me > 0)
        def _():
            backs(h, False).start()

        def keep(b, carry):
            dk[h, rows_of(b), :] = (dka[rows_of(HB + b), :] * SCALE).astype(BF)
            dv[h, rows_of(b), :] = dva[rows_of(HB + b), :].astype(BF)
            return carry

        lax.fori_loop(0, blocks, keep, 0)
        clear()
        for copy in stores(h, (0, 1)):
            copy.start()

    def finish(h):
        @pl.when(me > 0)
        def _():
            backs(h, True).wait_recv()
            for i, x in enumerate((dk, dv)):
                x[h, 0:RIM, :] = (x[h, 0:RIM, :].astype(F32) + rim_fl[h, i].astype(F32)).astype(BF)

        @pl.when(me < last)
        def _():
            backs(h, False).wait_recv()
            end = slice(tokens - RIM, tokens)
            for i, x in enumerate((dk, dv)):
                x[h, end, :] = (x[h, end, :].astype(F32) + rim_fr[h, i].astype(F32)).astype(BF)

        hub_sum[...] = chain_total(hub_back, h)

        def add(b, carry):
            ons = on_block(b)
            for i, x in enumerate((dk, dv)):
                out = x[h, rows_of(b), :].astype(F32)
                for j in range(G):
                    out = out + ons[j] * hub_sum[i, ENTRY[j], :]
                x[h, rows_of(b), :] = out.astype(BF)
            return carry

        lax.fori_loop(0, blocks, add, 0)
        for copy in stores(h, (2, 3)):
            copy.start()

    def table(b, carry):
        listed = lists_ref.shape[0]
        at = me * blocks + b
        for e in range(WIN):
            r = e - HB
            count = jnp.int32(0)
            for j in range(listed):
                count = count + jnp.where(lists_ref[j, at] == r, 1, 0)
            alive = (at + r >= 0) & (at + r < blocks * (last + 1))
            value = jnp.float32(DEAD)
            for n in range(1, listed + 1):
                value = jnp.where(alive & (count == n), jnp.float32(math.log2(n)), value)
            bias[b, e] = value
        return carry

    barrier = pltpu.get_barrier_semaphore()

    @pl.when(me > 0)
    def _():
        pl.semaphore_signal(barrier, inc=1, device_id={"ctx": me - 1}, device_id_type=MESH)

    @pl.when(me < last)
    def _():
        pl.semaphore_signal(barrier, inc=1, device_id={"ctx": me + 1}, device_id_type=MESH)

    for copy in wholes():
        copy.start()

    def load_all(h, carry):
        for copy in loads(h):
            copy.start()
        return carry

    lax.fori_loop(0, heads, load_all, 0)

    @pl.when((me > 0) & (me < last))
    def _():
        pl.semaphore_wait(barrier, 2)

    @pl.when((me == 0) | (me == last))
    def _():
        pl.semaphore_wait(barrier, 1)

    def open_head(h):
        for copy in loads(h):
            copy.wait()

    def when_in(d):
        return jnp.where(d > 0, jnp.minimum(IN_AT + IN_GAP * (d - 1), 2 * half - 1), 0)

    def when_back(d):
        return jnp.where(d > 0, jnp.minimum(BACK_AT + BACK_GAP * (d - 1), BACK_END), -1)

    in_right, in_left = when_in(me), when_in(last - me)
    back_right, back_left = when_back(me), when_back(last - me)

    for copy in wholes():
        copy.wait()
    pick()
    near(hub_in, 0)
    open_head(0)
    send_rims(0)
    if heads > 1:
        both(hub_in, 1, me == 0, me == last)
    lax.fori_loop(0, blocks, table, 0)

    def turn_first(b, carry):
        turn(0, 0, b)
        return carry

    inside = (me > 0) & (me < last)

    @pl.when(inside)
    def _():
        far(hub_in, 0)

    lax.fori_loop(0, blocks, turn_first, 0)

    @pl.when((me == 0) | (me == last))
    def _():
        far(hub_in, 0)

    if heads > 1:
        open_head(1)
        send_rims(1)
    clear()
    corners()
    assemble(0)
    scores(0, 0, 0)
    softmax(0, 0)
    scores(0, 1, 1)

    def head(h, carry):
        more = h + 1 < heads
        ahead = jnp.minimum(h + 1, heads - 1)

        def pair(i, carry):
            two = h + 2 < heads
            opening = more & (h == 0) & (i == 0)
            both(hub_in, h + 1, opening & (me > 0) & (in_right < half), opening & (me < last) & (in_left < half))
            both(hub_in, h + 2, two & (i == in_right), two & (i == in_left))
            late = i + half
            both(hub_in, h + 1, more & (late == in_right), more & (late == in_left))
            both(hub_back, h - 1, (h > 0) & (i == back_right), (h > 0) & (i == back_left))
            both(hub_back, h - 2, (h > 1) & (late == back_right), (h > 1) & (late == back_left))

            @pl.when((h > 1) & (i == half - 3))
            def _():
                finish(h - 2)

            @pl.when((h + 2 < heads) & (i == half // 2))
            def _():
                open_head(h + 2)
                send_rims(h + 2)

            @pl.when(more)
            def _():
                turn(h + 1, (h + 1) % 2, 2 * i)
                turn(h + 1, (h + 1) % 2, 2 * i + 1)

            @pl.when(more & (i == half - 1))
            def _():
                assemble(h + 1)

            b = 2 * i
            ends = i == half - 1
            h_next = jnp.where(ends, ahead, h)
            b_next = jnp.where(ends, 0, b + 2)
            softmax(b + 1, 1)
            products(h, b)
            scores(h_next, b_next, 0)
            scores(h_next, b_next + 1, 1)
            softmax(b_next, 0)
            return carry

        lax.fori_loop(0, half, pair, 0)
        deliver(h)
        return carry

    lax.fori_loop(0, heads, head, 0)
    both(hub_back, heads - 1, (me > 0) & (me <= last - me), (me < last) & (me > last - me))
    @pl.when(inside)
    def _():
        far(hub_back, heads - 1)

    if heads > 1:
        both(hub_back, heads - 2, back_right >= half, back_left >= half)
        finish(heads - 2)

    @pl.when((me == 0) | (me == last))
    def _():
        far(hub_back, heads - 1)

    finish(heads - 1)

    def close(h, carry):
        for copy in stores(h):
            copy.wait()

        @pl.when(me < last)
        def _():
            for copy in rims(h, True):
                copy.wait_send()
            backs(h, True).wait_send()
            for i in range(2):
                hop(hub_in, h, True, i).wait_send()
            for i in range(2):
                hop(hub_back, h, True, i).wait_send()

        @pl.when(me > 0)
        def _():
            for copy in rims(h, False):
                copy.wait_send()
            backs(h, False).wait_send()
            for i in range(2):
                hop(hub_in, h, False, i).wait_send()
            for i in range(2):
                hop(hub_back, h, False, i).wait_send()

        return carry

    lax.fori_loop(0, heads, close, 0)


def write_kernel(*refs):
    held, come, go = refs[8:]
    rows = refs[0].shape[0] // PARTS

    def pair(i, j):
        part = pl.ds(j * rows, rows)
        return (
            pltpu.make_async_copy(refs[i].at[part], held.at[i, part], come.at[i, j]),
            pltpu.make_async_copy(held.at[i, part], refs[4 + i].at[part], go.at[i, j]),
        )

    pairs = [pair(i, j) for i in range(4) for j in range(PARTS)]
    for load, _ in pairs:
        load.start()
    for load, store in pairs:
        load.wait()
        store.start()
    for _, store in pairs:
        store.wait()


def local(query_rows, key_rows, value_rows, out_grad, hub_blocks, local_lists):
    tokens, columns = query_rows.shape
    heads = columns // DH
    store = tokens + 2 * RIM + G * BLK
    blocks = tokens // BLK
    big = jax.ShapeDtypeStruct(query_rows.shape, BF)
    anywhere = pl.BlockSpec(memory_space=pl.ANY)
    smem = pl.BlockSpec(memory_space=pltpu.SMEM)
    vmem = pltpu.VMEM
    hub_shape = vmem((heads, 2, G * BLK, DH), BF)
    rim_shape = vmem((heads, 2, RIM, DH), BF)
    dma = pltpu.SemaphoreType.DMA
    units = 6 * heads * blocks * NE
    results = pl.pallas_call(
        layer_kernel,
        out_shape=[big] * 4,
        in_specs=[smem] * 2 + [anywhere] * 6,
        out_specs=[anywhere] * 4,
        scratch_shapes=[vmem((heads, store, DH), BF)] * 2
        + [vmem((heads, tokens, DH), BF)] * 2
        + [vmem((blocks, BLK, columns), BF)] * 2
        + [vmem((2, DH, store), BF)] * 2
        + [vmem((2, blocks, DH, BLK), BF)] * 2
        + [vmem((store, DH), F32)] * 2
        + [pltpu.SMEM((blocks, 8), F32)]
        + [vmem((heads, tokens, DH), BF)] * 4
        + [hub_shape] * 10
        + [vmem((2, G * BLK, DH), F32)]
        + [rim_shape] * 4
        + [vmem((NE * BLK, BLK), F32)] * 4
        + [vmem((8, BLK), F32)] * 2
        + [vmem(((NE + 1) * BLK, 2 * BLK), BF)] * 2
        + [dma((2,)), dma((4, heads)), dma((4, heads))]
        + [dma((2, 2, heads))] * 4
        + [dma((2, heads))] * 2
        + [dma((2, 2, heads))] * 2,
        compiler_params=pltpu.CompilerParams(
            collective_id=0, has_side_effects=True, vmem_limit_bytes=56 << 20
        ),
        cost_estimate=pl.CostEstimate(
            flops=units * 2 * BLK * BLK * DH,
            bytes_accessed=16 * tokens * columns,
            transcendentals=heads * blocks * NE * BLK * BLK,
        ),
        name="layer",
    )(
        hub_blocks, local_lists.T, query_rows, key_rows, value_rows, out_grad,
        key_rows.reshape(blocks, BLK, columns), value_rows.reshape(blocks, BLK, columns),
    )
    return pl.pallas_call(
        write_kernel,
        out_shape=[big] * 4,
        in_specs=[anywhere] * 4,
        out_specs=[anywhere] * 4,
        scratch_shapes=[vmem((4, tokens, columns), BF), dma((4, PARTS)), dma((4, PARTS))],
        compiler_params=pltpu.CompilerParams(vmem_limit_bytes=60 << 20),
        name="write",
    )(*results)


def solution(mesh):
    spec = P("ctx", "head")
    return jax.shard_map(
        local,
        mesh=mesh,
        in_specs=(spec, spec, spec, spec, P(), P()),
        out_specs=(spec, spec, spec, spec),
        check_vma=False,
    )
```

```python
import functools
import math

import jax
import jax.numpy as jnp
from jax import lax
from jax.experimental import pallas as pl
from jax.experimental.pallas import tpu as pltpu
from jax.sharding import PartitionSpec as P

DH = 128
BLK = 128
HB = 3
G = 2
WIN = 2 * HB + 1
NE = WIN + G
RIM = HB * BLK
DEAD = -1e30
PARTS = 4
IN_AT, IN_GAP = 6, 5
BACK_AT, BACK_GAP, BACK_END = 3, 4, 12
SCALE = 1.0 / math.sqrt(DH)
C = SCALE * math.log2(math.e)
F32 = jnp.float32
BF = jnp.bfloat16
MESH = pl.DeviceIdType.MESH
ENTRY = [slice(e * BLK, (e + 1) * BLK) for e in range(NE)]


def dot(a, b):
    return jnp.dot(a, b, preferred_element_type=F32)


def fold(x, op):
    return op(x.reshape(x.shape[0] // 8, 8, x.shape[1]), axis=0)


def rows_of(b, n=1):
    return pl.ds(pl.multiple_of(b * BLK, BLK), n * BLK)


def cols_of(h):
    return pl.ds(pl.multiple_of(h * DH, DH), DH)


def layer_kernel(
    hub_ref, lists_ref, q_ref, k_ref, v_ref, g_ref, k3_ref, v3_ref, att_out, dq_out, dk_out, dv_out,
    kx, vx, qx, gx, ko, vo, kt, vt, qt, gt, dka, dva, bias, att, dq, dk, dv,
    hub_own, hub_fl, hub_fr, hub_tr, hub_tl,
    hg_own, hg_fl, hg_fr, hg_tr, hg_tl, hub_sum,
    rim_tl, rim_tr, rim_fl, rim_fr,
    s0, s1, p0, p1, m0, m1, W, L,
    whole_sem, load_sem, store_sem, rim_send, rim_recv, hub_send, hub_recv,
    back_send, back_recv, hg_send, hg_recv,
):
    heads, tokens, _ = qx.shape
    blocks = tokens // BLK
    extended = blocks + 2 * HB
    half = blocks // 2
    me = lax.axis_index("ctx")
    last = lax.axis_size("ctx") - 1
    own = pl.ds(RIM, tokens)
    hubs = slice(extended * BLK, (extended + G) * BLK)
    right_rim = slice((HB + blocks) * BLK, extended * BLK)
    S, PU, M = (s0, s1), (p0, p1), (m0, m1)

    def loads(h):
        pairs = (
            (k_ref, kx.at[h, own]), (v_ref, vx.at[h, own]),
            (q_ref, qx.at[h]), (g_ref, gx.at[h]),
        )
        return [
            pltpu.make_async_copy(src.at[:, cols_of(h)], dst, load_sem.at[i, h])
            for i, (src, dst) in enumerate(pairs)
        ]

    def wholes():
        return [
            pltpu.make_async_copy(src, dst, whole_sem.at[i])
            for i, (src, dst) in enumerate(((k3_ref, ko), (v3_ref, vo)))
        ]

    def stores(h, which=range(4)):
        pairs = ((att, att_out), (dq, dq_out), (dk, dk_out), (dv, dv_out))
        return [
            pltpu.make_async_copy(src.at[h], dst.at[:, cols_of(h)], store_sem.at[i, h])
            for i, (src, dst) in enumerate(pairs)
            if i in which
        ]

    def remote(src, dst, send, recv, to):
        return pltpu.make_async_remote_copy(
            src_ref=src, dst_ref=dst, send_sem=send, recv_sem=recv,
            device_id={"ctx": to}, device_id_type=MESH,
        )

    def rims(h, right):
        source = pl.ds(blocks * BLK, RIM) if right else pl.ds(RIM, RIM)
        target = pl.ds(0, RIM) if right else right_rim
        d = 0 if right else 1
        to = me + 1 if right else me - 1
        return [
            remote(x.at[h, source], x.at[h, target], rim_send.at[d, i, h], rim_recv.at[d, i, h], to)
            for i, x in enumerate((kx, vx))
        ]

    def backs(h, right):
        if right:
            return remote(rim_tr.at[h], rim_fl.at[h], back_send.at[0, h], back_recv.at[0, h], me + 1)
        return remote(rim_tl.at[h], rim_fr.at[h], back_send.at[1, h], back_recv.at[1, h], me - 1)

    hub_in = (hub_own, hub_fl, hub_fr, hub_tr, hub_tl, hub_send, hub_recv)
    hub_back = (hg_own, hg_fl, hg_fr, hg_tr, hg_tl, hg_send, hg_recv)

    def hop(chain, h, right, i, source=None):
        mine, fl, fr, tr, tl, send, recv = chain
        d = 0 if right else 1
        land, to = (fl, me + 1) if right else (fr, me - 1)
        if source is None:
            source = tr if right else tl
        return remote(source.at[h, i], land.at[h, i], send.at[d, i, h], recv.at[d, i, h], to)

    def step(chain, h, right):
        mine, fl, fr, tr, tl = chain[:5]
        first, final = (0, last) if right else (last, 0)
        got, sent = (fl, tr) if right else (fr, tl)
        for i in range(2):
            @pl.when(me == first)
            def _():
                hop(chain, h, right, i, mine).start()

            @pl.when(me != first)
            def _():
                hop(chain, h, right, i).wait_recv()

            @pl.when((me != first) & (me != final))
            def _():
                sent[h, i] = mine[h, i] + got[h, i]
                hop(chain, h, right, i).start()

    def both(chain, h, right, left):
        @pl.when(right)
        def _():
            step(chain, h, True)

        @pl.when(left)
        def _():
            step(chain, h, False)

    def near(chain, h):
        @pl.when(me <= last - me)
        def _():
            step(chain, h, True)

        @pl.when(me > last - me)
        def _():
            step(chain, h, False)

    def far(chain, h):
        @pl.when(me <= last - me)
        def _():
            step(chain, h, False)

        @pl.when(me > last - me)
        def _():
            step(chain, h, True)

    def chain_total(chain, h):
        mine, fl, fr = chain[:3]
        total = mine[h].astype(F32)
        total = total + jnp.where(me > 0, fl[h].astype(F32), 0.0)
        return total + jnp.where(me < last, fr[h].astype(F32), 0.0)

    def on_block(b):
        return [jnp.where(hub_ref[j] - me * blocks == b, 1.0, 0.0).astype(F32) for j in range(G)]

    def send_rims(h):
        @pl.when(me < last)
        def _():
            for copy in rims(h, True):
                copy.start()

        @pl.when(me > 0)
        def _():
            for copy in rims(h, False):
                copy.start()

    def pick():
        for j in range(G):
            spot = hub_ref[j] - me * blocks
            here = jnp.where((spot >= 0) & (spot < blocks), 1.0, 0.0).astype(F32)
            at = jnp.clip(spot, 0, blocks - 1)
            for i, x in enumerate((ko, vo)):
                block = (x[at].astype(F32) * here).astype(BF)
                for h in range(heads):
                    hub_own[h, i, ENTRY[j], :] = block[:, h * DH : (h + 1) * DH]

    def turn(h, slot, b):
        r = rows_of(b)
        e = rows_of(HB + b)
        qt[slot, b] = qx[h, r, :].T
        gt[slot, b] = gx[h, r, :].T
        kt[slot, :, e] = kx[h, e, :].T
        vt[slot, :, e] = vx[h, e, :].T

    def assemble(h):
        @pl.when(me > 0)
        def _():
            for copy in rims(h, True):
                copy.wait_recv()

        @pl.when(me == 0)
        def _():
            kx[h, 0:RIM, :] = jnp.zeros((RIM, DH), BF)
            vx[h, 0:RIM, :] = jnp.zeros((RIM, DH), BF)

        @pl.when(me < last)
        def _():
            for copy in rims(h, False):
                copy.wait_recv()

        @pl.when(me == last)
        def _():
            kx[h, right_rim, :] = jnp.zeros((RIM, DH), BF)
            vx[h, right_rim, :] = jnp.zeros((RIM, DH), BF)

        mine, fl, fr = hub_in[:3]
        for i, x in enumerate((kx, vx)):
            total = mine[h, i]
            total = total + jnp.where(me > 0, fl[h, i], jnp.zeros_like(total))
            total = total + jnp.where(me < last, fr[h, i], jnp.zeros_like(total))
            x[h, hubs, :] = total
        slot = h % 2
        for x, t in ((kx, kt), (vx, vt)):
            for e in list(range(HB)) + list(range(HB + blocks, extended + G)):
                es = slice(e * BLK, (e + 1) * BLK)
                t[slot, :, es] = x[h, es, :].T

    def scores(h, b, n):
        slot = h % 2
        qt_b, gt_b = qt[slot, b], gt[slot, b]
        window = rows_of(b, WIN)
        s_local = dot(kx[h, window, :], qt_b)
        s_hub = dot(kx[h, hubs, :], qt_b)
        S[n][: WIN * BLK, :] = s_local
        S[n][WIN * BLK :, :] = s_hub
        PU[n][: WIN * BLK, :] = dot(vx[h, window, :], gt_b)
        PU[n][WIN * BLK :, :] = dot(vx[h, hubs, :], gt_b)
        tops = [fold(s_local[ENTRY[e]], jnp.max) * C + bias[b, e] for e in range(WIN)]
        tops += [fold(s_hub[ENTRY[e]], jnp.max) * C for e in range(G)]
        M[n][...] = functools.reduce(jnp.maximum, tops)

    def softmax(b, n):
        shift = [bias[b, e] for e in range(WIN)] + [0.0] * G
        top = jnp.max(M[n][...], axis=0, keepdims=True)
        ps = [jnp.exp2(S[n][ENTRY[e], :] * C + (shift[e] - top)) for e in range(NE)]
        total = functools.reduce(jnp.add, [fold(p, jnp.sum) for p in ps])
        moved = functools.reduce(
            jnp.add, [fold(ps[e] * PU[n][ENTRY[e], :], jnp.sum) for e in range(NE)]
        )
        inverse = 1.0 / jnp.sum(total, axis=0, keepdims=True)
        offset = jnp.sum(moved, axis=0, keepdims=True) * inverse
        for e in range(NE):
            chances = ps[e] * inverse
            at = e + n if e < WIN else e + 1
            place = (slice(at * BLK, (at + 1) * BLK), slice(n * BLK, (n + 1) * BLK))
            W[place] = chances.astype(BF)
            L[place] = (chances * (PU[n][ENTRY[e], :] - offset)).astype(BF)

    def products(h, b):
        slot = h % 2
        r = rows_of(b, 2)
        window = rows_of(b, WIN + 1)
        local = slice(0, (WIN + 1) * BLK)
        hub = slice((WIN + 1) * BLK, (NE + 1) * BLK)
        mixed = dot(vt[slot, :, window], W[local, :]) + dot(vt[slot, :, hubs], W[hub, :])
        att[h, r, :] = mixed.T.astype(BF)
        grad = dot(kt[slot, :, window], L[local, :]) + dot(kt[slot, :, hubs], L[hub, :])
        dq[h, r, :] = (grad * SCALE).T.astype(BF)
        for n in range(2):
            lanes = slice(n * BLK, (n + 1) * BLK)
            mine = slice(n * BLK, (n + WIN) * BLK)
            q, g = qx[h, rows_of(b + n), :], gx[h, rows_of(b + n), :]
            dka[rows_of(b + n, WIN), :] += dot(L[mine, lanes], q)
            dka[hubs, :] += dot(L[hub, lanes], q)
            dva[rows_of(b + n, WIN), :] += dot(W[mine, lanes], g)
            dva[hubs, :] += dot(W[hub, lanes], g)

    def corners():
        for x in (W, L):
            x[0:BLK, BLK : 2 * BLK] = jnp.zeros((BLK, BLK), BF)
            x[WIN * BLK : (WIN + 1) * BLK, 0:BLK] = jnp.zeros((BLK, BLK), BF)

    def clear():
        dka[...] = jnp.zeros(dka.shape, F32)
        dva[...] = jnp.zeros(dva.shape, F32)

    def deliver(h):
        for i, (acc, scale) in enumerate(((dka, SCALE), (dva, 1.0))):
            rim_tl[h, i] = (acc[0:RIM, :] * scale).astype(BF)
            rim_tr[h, i] = (acc[right_rim, :] * scale).astype(BF)
            hg_own[h, i] = (acc[hubs, :] * scale).astype(BF)
        both(hub_back, h, me == 0, me == last)

        @pl.when(me < last)
        def _():
            backs(h, True).start()

        @pl.when(me > 0)
        def _():
            backs(h, False).start()

        def keep(b, carry):
            dk[h, rows_of(b), :] = (dka[rows_of(HB + b), :] * SCALE).astype(BF)
            dv[h, rows_of(b), :] = dva[rows_of(HB + b), :].astype(BF)
            return carry

        lax.fori_loop(0, blocks, keep, 0)
        clear()
        for copy in stores(h, (0, 1)):
            copy.start()

    def finish(h):
        @pl.when(me > 0)
        def _():
            backs(h, True).wait_recv()
            for i, x in enumerate((dk, dv)):
                x[h, 0:RIM, :] = (x[h, 0:RIM, :].astype(F32) + rim_fl[h, i].astype(F32)).astype(BF)

        @pl.when(me < last)
        def _():
            backs(h, False).wait_recv()
            end = slice(tokens - RIM, tokens)
            for i, x in enumerate((dk, dv)):
                x[h, end, :] = (x[h, end, :].astype(F32) + rim_fr[h, i].astype(F32)).astype(BF)

        hub_sum[...] = chain_total(hub_back, h)

        def add(b, carry):
            ons = on_block(b)
            for i, x in enumerate((dk, dv)):
                out = x[h, rows_of(b), :].astype(F32)
                for j in range(G):
                    out = out + ons[j] * hub_sum[i, ENTRY[j], :]
                x[h, rows_of(b), :] = out.astype(BF)
            return carry

        lax.fori_loop(0, blocks, add, 0)
        for copy in stores(h, (2, 3)):
            copy.start()

    def table(b, carry):
        listed = lists_ref.shape[0]
        at = me * blocks + b
        for e in range(WIN):
            r = e - HB
            count = jnp.int32(0)
            for j in range(listed):
                count = count + jnp.where(lists_ref[j, at] == r, 1, 0)
            alive = (at + r >= 0) & (at + r < blocks * (last + 1))
            value = jnp.float32(DEAD)
            for n in range(1, listed + 1):
                value = jnp.where(alive & (count == n), jnp.float32(math.log2(n)), value)
            bias[b, e] = value
        return carry

    barrier = pltpu.get_barrier_semaphore()

    @pl.when(me > 0)
    def _():
        pl.semaphore_signal(barrier, inc=1, device_id={"ctx": me - 1}, device_id_type=MESH)

    @pl.when(me < last)
    def _():
        pl.semaphore_signal(barrier, inc=1, device_id={"ctx": me + 1}, device_id_type=MESH)

    for copy in wholes():
        copy.start()

    def load_all(h, carry):
        for copy in loads(h):
            copy.start()
        return carry

    lax.fori_loop(0, heads, load_all, 0)

    @pl.when((me > 0) & (me < last))
    def _():
        pl.semaphore_wait(barrier, 2)

    @pl.when((me == 0) | (me == last))
    def _():
        pl.semaphore_wait(barrier, 1)

    def open_head(h):
        for copy in loads(h):
            copy.wait()

    def when_in(d):
        return jnp.where(d > 0, jnp.minimum(IN_AT + IN_GAP * (d - 1), 2 * half - 1), 0)

    def when_back(d):
        return jnp.where(d > 0, jnp.minimum(BACK_AT + BACK_GAP * (d - 1), BACK_END), -1)

    in_right, in_left = when_in(me), when_in(last - me)
    back_right, back_left = when_back(me), when_back(last - me)

    for copy in wholes():
        copy.wait()
    pick()
    near(hub_in, 0)
    open_head(0)
    send_rims(0)
    if heads > 1:
        both(hub_in, 1, me == 0, me == last)
    lax.fori_loop(0, blocks, table, 0)

    def turn_first(b, carry):
        turn(0, 0, b)
        return carry

    inside = (me > 0) & (me < last)

    @pl.when(inside)
    def _():
        far(hub_in, 0)

    lax.fori_loop(0, blocks, turn_first, 0)

    @pl.when((me == 0) | (me == last))
    def _():
        far(hub_in, 0)

    if heads > 1:
        open_head(1)
        send_rims(1)
    clear()
    corners()
    assemble(0)
    scores(0, 0, 0)
    softmax(0, 0)
    scores(0, 1, 1)

    def head(h, carry):
        more = h + 1 < heads
        ahead = jnp.minimum(h + 1, heads - 1)

        def pair(i, carry):
            two = h + 2 < heads
            opening = more & (h == 0) & (i == 0)
            both(hub_in, h + 1, opening & (me > 0) & (in_right < half), opening & (me < last) & (in_left < half))
            both(hub_in, h + 2, two & (i == in_right), two & (i == in_left))
            late = i + half
            both(hub_in, h + 1, more & (late == in_right), more & (late == in_left))
            both(hub_back, h - 1, (h > 0) & (i == back_right), (h > 0) & (i == back_left))
            both(hub_back, h - 2, (h > 1) & (late == back_right), (h > 1) & (late == back_left))

            @pl.when((h > 1) & (i == half - 3))
            def _():
                finish(h - 2)

            @pl.when((h + 2 < heads) & (i == half // 2))
            def _():
                open_head(h + 2)
                send_rims(h + 2)

            @pl.when(more)
            def _():
                turn(h + 1, (h + 1) % 2, 2 * i)
                turn(h + 1, (h + 1) % 2, 2 * i + 1)

            @pl.when(more & (i == half - 1))
            def _():
                assemble(h + 1)

            b = 2 * i
            ends = i == half - 1
            h_next = jnp.where(ends, ahead, h)
            b_next = jnp.where(ends, 0, b + 2)
            softmax(b + 1, 1)
            products(h, b)
            scores(h_next, b_next, 0)
            scores(h_next, b_next + 1, 1)
            softmax(b_next, 0)
            return carry

        lax.fori_loop(0, half, pair, 0)
        deliver(h)
        return carry

    lax.fori_loop(0, heads, head, 0)
    both(hub_back, heads - 1, (me > 0) & (me <= last - me), (me < last) & (me > last - me))
    @pl.when(inside)
    def _():
        far(hub_back, heads - 1)

    if heads > 1:
        both(hub_back, heads - 2, back_right >= half, back_left >= half)
        finish(heads - 2)

    @pl.when((me == 0) | (me == last))
    def _():
        far(hub_back, heads - 1)

    finish(heads - 1)

    def close(h, carry):
        for copy in stores(h):
            copy.wait()

        @pl.when(me < last)
        def _():
            for copy in rims(h, True):
                copy.wait_send()
            backs(h, True).wait_send()
            for i in range(2):
                hop(hub_in, h, True, i).wait_send()
            for i in range(2):
                hop(hub_back, h, True, i).wait_send()

        @pl.when(me > 0)
        def _():
            for copy in rims(h, False):
                copy.wait_send()
            backs(h, False).wait_send()
            for i in range(2):
                hop(hub_in, h, False, i).wait_send()
            for i in range(2):
                hop(hub_back, h, False, i).wait_send()

        return carry

    lax.fori_loop(0, heads, close, 0)


def write_kernel(*refs):
    held, come, go = refs[8:]
    rows = refs[0].shape[0] // PARTS

    def pair(i, j):
        part = pl.ds(j * rows, rows)
        return (
            pltpu.make_async_copy(refs[i].at[part], held.at[i, part], come.at[i, j]),
            pltpu.make_async_copy(held.at[i, part], refs[4 + i].at[part], go.at[i, j]),
        )

    pairs = [pair(i, j) for i in range(4) for j in range(PARTS)]
    for load, _ in pairs:
        load.start()
    for load, store in pairs:
        load.wait()
        store.start()
    for _, store in pairs:
        store.wait()


def local(query_rows, key_rows, value_rows, out_grad, hub_blocks, local_lists):
    tokens, columns = query_rows.shape
    heads = columns // DH
    store = tokens + 2 * RIM + G * BLK
    blocks = tokens // BLK
    big = jax.ShapeDtypeStruct(query_rows.shape, BF)
    anywhere = pl.BlockSpec(memory_space=pl.ANY)
    smem = pl.BlockSpec(memory_space=pltpu.SMEM)
    vmem = pltpu.VMEM
    hub_shape = vmem((heads, 2, G * BLK, DH), BF)
    rim_shape = vmem((heads, 2, RIM, DH), BF)
    dma = pltpu.SemaphoreType.DMA
    units = 6 * heads * blocks * NE
    results = pl.pallas_call(
        layer_kernel,
        out_shape=[big] * 4,
        in_specs=[smem] * 2 + [anywhere] * 6,
        out_specs=[anywhere] * 4,
        scratch_shapes=[vmem((heads, store, DH), BF)] * 2
        + [vmem((heads, tokens, DH), BF)] * 2
        + [vmem((blocks, BLK, columns), BF)] * 2
        + [vmem((2, DH, store), BF)] * 2
        + [vmem((2, blocks, DH, BLK), BF)] * 2
        + [vmem((store, DH), F32)] * 2
        + [pltpu.SMEM((blocks, 8), F32)]
        + [vmem((heads, tokens, DH), BF)] * 4
        + [hub_shape] * 10
        + [vmem((2, G * BLK, DH), F32)]
        + [rim_shape] * 4
        + [vmem((NE * BLK, BLK), F32)] * 4
        + [vmem((8, BLK), F32)] * 2
        + [vmem(((NE + 1) * BLK, 2 * BLK), BF)] * 2
        + [dma((2,)), dma((4, heads)), dma((4, heads))]
        + [dma((2, 2, heads))] * 4
        + [dma((2, heads))] * 2
        + [dma((2, 2, heads))] * 2,
        compiler_params=pltpu.CompilerParams(
            collective_id=0, has_side_effects=True, vmem_limit_bytes=56 << 20
        ),
        cost_estimate=pl.CostEstimate(
            flops=units * 2 * BLK * BLK * DH,
            bytes_accessed=16 * tokens * columns,
            transcendentals=heads * blocks * NE * BLK * BLK,
        ),
        name="layer",
    )(
        hub_blocks, local_lists.T, query_rows, key_rows, value_rows, out_grad,
        key_rows.reshape(blocks, BLK, columns), value_rows.reshape(blocks, BLK, columns),
    )
    return pl.pallas_call(
        write_kernel,
        out_shape=[big] * 4,
        in_specs=[anywhere] * 4,
        out_specs=[anywhere] * 4,
        scratch_shapes=[vmem((4, tokens, columns), BF), dma((4, PARTS)), dma((4, PARTS))],
        compiler_params=pltpu.CompilerParams(vmem_limit_bytes=60 << 20),
        name="write",
    )(*results)


def solution(mesh):
    spec = P("ctx", "head")
    return jax.shard_map(
        local,
        mesh=mesh,
        in_specs=(spec, spec, spec, spec, P(), P()),
        out_specs=(spec, spec, spec, spec),
        check_vma=False,
    )
```
